128 devices in a mesh: gen: 32 (over y, z, core), grp: 4 (over x).
Axes of the slice: x: 4, y: 4, z: 4, core: 2. Of those that a mesh axis runs over, the one named last changes fastest.
Arguments:
- query_in: bfloat16 [4, 4096, 4096], P('grp', 'gen'), may hold values from -8 to 8, as said below
- key_in: bfloat16 [4, 4096, 4096], P('grp', 'gen'), may hold values from -8 to 8
- value_in: bfloat16 [4, 4096, 4096], P('grp', 'gen'), may hold values from -6 to 6
- teacher_w: bfloat16 [4096, 5120], P('gen'), may hold values from -0.09375 to 0.09375
- disc_heads: float32 [8, 5120], replicated, may hold values from -0.078125 to 0.078125
- frame_of_token: int32 [4, 4096], P('grp'), may hold values from 0 to 20, never falling along the last dimension, each value on 1 to 390 neighbouring positions
- head_of_frame: int32 [4, 21], P('grp'), may hold values from 0 to 7
- timestep: int32 [4], P('grp'), may hold values from 0 to 999
Outputs:
- latents: bfloat16 [4, 4096, 4096], P('grp', 'gen')
- grad_query: bfloat16 [4, 4096, 4096], P('grp', 'gen')
- grad_key: bfloat16 [4, 4096, 4096], P('grp', 'gen')
- grad_value: bfloat16 [4, 4096, 4096], P('grp', 'gen')
- grad_heads: float32 [8, 5120], replicated
The draws below stay inside these ranges and needn't reach their ends.
Inputs may be any that keep to these rules, and one draw needn't show every extreme that they name: `query_in`: entries lie within the range; in some draws a few queries equal some keys. `frame_of_token`: within a clip the frame numbers never fall along the tokens; every frame holds 1 to 390 tokens and some frame exactly 390.
All inputs are finite; a program needn't handle non-finite values.
Results may differ from the reference program's by a relative error of at most 0.035.
Values may be sent and summed in bfloat16 or wider, within the bound.
A program may use at most 64 MiB of HBM per device.

```python
import math
import jax
import jax.numpy as jnp
import numpy as np
from jax import lax

HEADS = 32
HS = 128
DH = 5120
FRAMES = 21
NDH = 8
NSTEPS = 1000
TOKENS = 4096
CLIPS = 4
WIDTH = 4096
FRAME_MOST = 390


def base_values(key, salt):
    draw_key = jax.random.fold_in(key, salt)
    values = jnp.clip(jax.random.normal(draw_key, (CLIPS, TOKENS, HEADS * HS), jnp.float32), -6.0, 6.0)
    return values


def draw_query_in(key, part):
    values = base_values(key, 3)
    return values.astype(jnp.bfloat16)


def draw_key_in(key, part):
    values = base_values(key, 5)
    return values.astype(jnp.bfloat16)


def set_ends(drawn, stream_key, smallest, top_value):
    longest = drawn.shape.index(max(drawn.shape))
    spots = []
    for shift in (0, 1):
        where = [jax.random.randint(jax.random.fold_in(stream_key, axis), (), 0, length) for axis, length in enumerate(drawn.shape)]
        where[longest] = (where[longest] + shift) % drawn.shape[longest]
        spots.append(tuple(where))
    return drawn.at[spots[0]].set(smallest).at[spots[1]].set(top_value)


def shard_levels(rng, dims, cuts, low, largest):
    level = 1.0
    for dim, parts in cuts:
        steps = jax.random.uniform(jax.random.fold_in(jax.random.fold_in(rng, 6), dim), (parts,), jnp.float32, low / len(cuts), largest / len(cuts))
        level = level * jnp.repeat(jnp.exp(steps), dims[dim] // parts).reshape((-1,) + (1,) * (len(dims) - 1 - dim))
    return level


def split_up(amount, total, most, slope):
    portions = [(1 << 20) // math.isqrt(rank ** slope) + 1 for rank in range(2, amount + 1)]
    spare, holding = total - most - (amount - 1), [1] * (amount - 1)
    while spare > 0:
        candidates = [i for i in range(amount - 1) if holding[i] < most]
        mass, budget = sum([portions[i] for i in candidates]), spare
        for i in candidates:
            addition = min(most - holding[i], max(1, budget * portions[i] // mass), spare)
            holding[i] = holding[i] + addition
            spare = spare - addition
    return np.array([most] + holding)


def ragged(stream_key, number_of, total, limit, skew):
    if number_of == 2:
        one = jax.random.randint(stream_key, (), max(1, total - limit), min(limit, total - 1) + 1)
        return jnp.stack([one, total - one])
    tallies = jnp.asarray(split_up(number_of, total, limit, skew), jnp.int32)
    couples = (number_of - 1) // 2
    giver, sink = tallies[1:1 + 2 * couples:2], tallies[2:2 + 2 * couples:2]
    slack = jnp.minimum(giver - 1, limit - sink)
    passed = jax.random.randint(jax.random.fold_in(stream_key, 1), (couples,), 0, 1 << 20) % (slack + 1)
    tallies = tallies.at[1:1 + 2 * couples:2].set(giver - passed).at[2:2 + 2 * couples:2].set(sink + passed)
    return tallies[jax.random.permutation(jax.random.fold_in(stream_key, 2), number_of)]


def scatter_about(own_key, shape, scale, most, cuts=(), kind=jnp.bfloat16):
    values = scale * jax.random.normal(own_key, shape, jnp.float32)
    if cuts:
        values = values * shard_levels(own_key, shape, cuts, -0.22, 0.18)
    return jnp.clip(values, -most, most).astype(kind)


def setup_inputs(seed: int = 0) -> dict:
    key_list = jax.random.split(jax.random.key(seed), 9)
    return {
        "query_in": draw_query_in(jax.random.fold_in(key_list[8], 71), 0),
        "key_in": draw_key_in(jax.random.fold_in(key_list[8], 71), 0),
        "value_in": scatter_about(key_list[2], (CLIPS, TOKENS, WIDTH), 1.0, 6.0, ((0, 4), (1, 32))),
        "teacher_w": scatter_about(key_list[3], (WIDTH, DH), WIDTH ** -0.5, 0.09375, ((0, 32),)),
        "disc_heads": scatter_about(key_list[4], (NDH, DH), DH ** -0.5, 0.078125, (), jnp.float32),
        "frame_of_token": jax.vmap(lambda own: jnp.searchsorted(jnp.cumsum(ragged(own, FRAMES, TOKENS, FRAME_MOST, 1)), jnp.arange(TOKENS), side="right"))(jax.random.split(key_list[5], CLIPS)).reshape((CLIPS, TOKENS)).astype(jnp.int32),
        "head_of_frame": set_ends(jax.random.randint(key_list[6], (CLIPS, FRAMES), 0, NDH), jax.random.fold_in(key_list[6], 1), 0, NDH - 1).astype(jnp.int32),
        "timestep": set_ends(jax.random.randint(key_list[7], (CLIPS,), 0, NSTEPS), jax.random.fold_in(key_list[7], 1), 0, NSTEPS - 1).astype(jnp.int32),
    }


epsilon = 1e-06

def attend(items):
    head_query, head_key, head_value = items
    inv_scale = 1.0 / math.sqrt(HS)
    scores = jnp.dot(head_query, head_key.T, preferred_element_type=jnp.float32) * inv_scale
    peak = lax.optimization_barrier(jnp.max(scores, axis=1, keepdims=True))
    weights = jnp.exp(scores - peak)
    total = lax.optimization_barrier(jnp.sum(weights, axis=1, keepdims=True))
    mixed = jnp.dot(weights.astype(jnp.bfloat16), head_value, preferred_element_type=jnp.float32) / total
    return (mixed.astype(jnp.bfloat16), (peak + jnp.log(total))[:, 0])

def attend_back(items):
    head_query, head_key, head_value, lse_rows, grad_rows, delta_rows = items
    inv_scale = 1.0 / math.sqrt(HS)
    scores = jnp.dot(head_query, head_key.T, preferred_element_type=jnp.float32) * inv_scale
    probs = jnp.exp(scores - lse_rows[:, None])
    grad_value = jnp.dot(probs.astype(jnp.bfloat16).T, grad_rows, preferred_element_type=jnp.float32)
    grad_probs = jnp.dot(grad_rows, head_value.T, preferred_element_type=jnp.float32)
    dscore = (probs * (grad_probs - delta_rows[:, None]) * inv_scale).astype(jnp.bfloat16)
    grad_query = jnp.dot(dscore, head_key, preferred_element_type=jnp.float32)
    grad_key = jnp.dot(dscore.T, head_query, preferred_element_type=jnp.float32)
    return (grad_query.astype(jnp.bfloat16), grad_key.astype(jnp.bfloat16), grad_value.astype(jnp.bfloat16))

def split_heads(array):
    return array.reshape(TOKENS, HEADS, HS).transpose(1, 0, 2)

def join_heads(array):
    return array.transpose(1, 0, 2).reshape(TOKENS, WIDTH)

def one_clip(items, teacher_w, disc_heads):
    query_clip, key_clip, value_clip, frames, head_index, tstep = items
    head_query = split_heads(query_clip)
    head_key = split_heads(key_clip)
    head_value = split_heads(value_clip)
    mixed, lse = lax.map(attend, (head_query, head_key, head_value))
    latent = join_heads(mixed)
    member = frames[None, :] == jnp.arange(FRAMES, dtype=jnp.int32)[:, None]
    counts = lax.optimization_barrier(jnp.sum(member.astype(jnp.float32), axis=1))
    pooled = jnp.dot(member.astype(jnp.bfloat16), latent, preferred_element_type=jnp.float32) / counts[:, None]
    squares = lax.optimization_barrier(jnp.sum(pooled * pooled, axis=1))
    projected = jnp.dot(pooled.astype(jnp.bfloat16), teacher_w, preferred_element_type=jnp.float32)
    root = jnp.sqrt(squares / WIDTH + epsilon)
    pre = projected / root[:, None]
    gate = jax.nn.sigmoid(pre)
    feature = pre * gate
    picked = (head_index[:, None] == jnp.arange(NDH, dtype=jnp.int32)[None, :]).astype(jnp.float32)
    head_rows = jnp.dot(picked, disc_heads, precision=lax.Precision.HIGHEST)
    score = lax.optimization_barrier(jnp.sum(feature * head_rows, axis=1))
    weight = (tstep.astype(jnp.float32) + 1.0) / NSTEPS
    grad_score = -weight * jax.nn.sigmoid(-score) / FRAMES
    grad_heads = jnp.dot(picked.T, grad_score[:, None] * feature, precision=lax.Precision.HIGHEST)
    grad_pre = grad_score[:, None] * head_rows * gate * (1.0 + pre * (1.0 - gate))
    grad_projected = (grad_pre / root[:, None]).astype(jnp.bfloat16)
    grad_root = -lax.optimization_barrier(jnp.sum(grad_pre * pre, axis=1)) / root
    grad_pooled = jnp.dot(grad_projected, teacher_w.T, preferred_element_type=jnp.float32) + (grad_root / root / WIDTH)[:, None] * pooled
    spread = grad_pooled / counts[:, None]
    grad_latent = (TOKENS * jnp.take(spread, frames, axis=0)).astype(jnp.bfloat16)
    product = grad_latent.astype(jnp.float32) * latent.astype(jnp.float32)
    delta = lax.optimization_barrier(jnp.sum(product.reshape(TOKENS, HEADS, HS), axis=2)).T
    grad_q, grad_k, grad_v = lax.map(attend_back, (head_query, head_key, head_value, lse, split_heads(grad_latent), delta))
    return (latent, join_heads(grad_q), join_heads(grad_k), join_heads(grad_v), grad_heads)

def reference(query_in, key_in, value_in, teacher_w, disc_heads, frame_of_token, head_of_frame, timestep):

    def clip_fn(items):
        return one_clip(items, teacher_w, disc_heads)
    latents, grad_query, grad_key, grad_value, head_terms = lax.map(clip_fn, (query_in, key_in, value_in, frame_of_token, head_of_frame, timestep))
    return (latents, grad_query, grad_key, grad_value, lax.optimization_barrier(jnp.sum(head_terms, axis=0)))
```

```python
import functools
import math

import jax
import jax.numpy as jnp
from jax import lax
from jax.experimental import pallas as pl
from jax.experimental.pallas import tpu as pltpu
from jax.sharding import PartitionSpec as P

HS = 128
FRAMES = 21
NDH = 8
NSTEPS = 1000
EPS = 1e-06
GEN = 32
GRP = 4
TOK = 4096
TD = 128
DH = 5120
FP = 32
OT = 256
OWN = 21
MESH = pl.DeviceIdType.MESH
f32 = jnp.float32
bf16 = jnp.bfloat16
NT = (((1,), (1,)), ((), ()))
NN = (((1,), (0,)), ((), ()))
TN = (((0,), (0,)), ((), ()))
CHIPS = [
    (2, 2), (3, 2), (2, 3), (1, 2), (2, 1), (0, 2), (2, 0), (3, 1), (1, 3), (3, 3), (1, 1),
    (0, 3), (0, 1), (3, 0), (1, 0),
]
FAR = [(dy, dz, dc) for dy, dz in CHIPS for dc in (0, 1)] + [(0, 0, 1)]


def mm(a, b, dims):
    return lax.dot_general(a, b, dims, preferred_element_type=f32)


def body(
    q_in, k_in, v_in, w_ref, disc_ref, frames_ref, hof_ref, time_ref,
    lat_out, dq_out, dk_out, dv_out, gh_out,
    probs, qh, kh, vh, oh, sa, sb, dkt, qwt, wrow, member, memberl, rbuf, r_all, g_src, g_all,
    rs_src, rs_recv, ag_src, proj, head_rows, gsf, hp_src, hp_all,
    sem_send, sem_q, sem_recv,
):
    g = lax.axis_index("gen")
    x = lax.axis_index("grp")
    y = g // 8
    z = (g // 2) % 4
    c = g % 2
    chip = g // 2

    def peer(off):
        dy, dz, dc = off
        ey = dy + c * (dz - dy)
        ez = dz + c * (dy - dz)
        return ((y + ey) % 4) * 8 + ((z + ez) % 4) * 2 + (c + dc) % 2

    def rows(i, n):
        return pl.ds(pl.multiple_of(i * n, n), n)

    def remote(src, dst, send, recv, dev):
        return pltpu.make_async_remote_copy(
            src_ref=src, dst_ref=dst, send_sem=send, recv_sem=recv,
            device_id={"gen": dev}, device_id_type=MESH,
        )

    def drain(ref, sem):
        pltpu.make_async_copy(ref, ref, sem).wait()

    barrier = pltpu.get_barrier_semaphore()
    for off in FAR:
        pl.semaphore_signal(barrier, inc=1, device_id={"gen": peer(off)}, device_id_type=MESH)
    for d in range(1, GRP):
        pl.semaphore_signal(
            barrier, inc=1, device_id={"grp": (x + d) % GRP}, device_id_type=MESH
        )
    pl.semaphore_wait(barrier, GEN - 1 + GRP - 1)

    for src, dst, which in ((k_in, kh, 0), (v_in, vh, 1)):
        pltpu.make_async_copy(src.at[:, rows(g, TD)], dst.at[rows(g, TD), :], sem_recv.at[which]).start()
        for off in FAR:
            p = peer(off)
            remote(
                src.at[:, rows(p, TD)], dst.at[rows(g, TD), :],
                sem_send.at[which], sem_recv.at[which], p,
            ).start()

    def q_chip(i, sign):
        dy = i % 4
        dz = (i // 4 + i) % 4
        return ((y + sign * dy + 4) % 4) * 4 + (z + sign * dz + 4) % 4

    pltpu.make_async_copy(q_in.at[:, rows(g, TD)], qh.at[rows(g, TD), :], sem_q.at[0]).start()
    for i in range(16):
        for dc in (0, 1):
            if i == 0 and dc == 0:
                continue
            p = q_chip(i, 1) * 2 + (c + dc) % 2
            remote(
                q_in.at[:, rows(p, TD)], qh.at[rows(g, TD), :], sem_send.at[2], sem_q.at[i], p
            ).start()

    frames = frames_ref[...]
    mem = (frames == lax.broadcasted_iota(jnp.int32, (FP, TOK), 0)).astype(f32)
    member[...] = mem.astype(bf16)
    counts = jnp.sum(mem, axis=1, keepdims=True)
    inv_count = jnp.where(counts > 0.0, 1.0 / jnp.maximum(counts, 1.0), 0.0)
    lane_n = lax.broadcasted_iota(jnp.int32, (FP, 128), 1)
    sub_n = lax.broadcasted_iota(jnp.int32, (FP, 128), 0)
    lane_8 = lax.broadcasted_iota(jnp.int32, (16, 128), 1)
    sub_8 = lax.broadcasted_iota(jnp.int32, (16, 128), 0)
    picked = jnp.zeros((FP, 128), f32)
    picked_t = jnp.zeros((16, 128), f32)
    for f in range(FRAMES):
        j = hof_ref[0, f]
        picked = jnp.where((sub_n == f) & (lane_n == j), 1.0, picked)
        picked_t = jnp.where((lane_8 == f) & (sub_8 == j), 1.0, picked_t)
    picked = picked[:, :NDH].astype(bf16)
    picked_t = picked_t[:, :FP].astype(bf16)
    for n in range(DH // 512):
        cols = pl.ds(n * 512, 512)
        part = disc_ref[:, cols]
        total = jnp.zeros((FP, 512), f32)
        for _ in range(3):
            high = part.astype(bf16)
            total = total + mm(picked, high, NN)
            part = part - high.astype(f32)
        head_rows[:, cols] = total

    scale2 = math.log2(math.e) / math.sqrt(HS)
    ck = 512
    bq = 256

    def step(i_s, s_write, i_p, s_read, peak):
        if i_s is not None:
            drain(qh.at[pl.ds(0, bq), :], sem_q.at[i_s])
            qb = qh[rows(q_chip(i_s, -1), bq), :]
            top = jnp.full((bq, 128), -jnp.inf, f32)
        if i_p is not None:
            ch = q_chip(i_p, -1)
            r = rows(ch, bq)
            l = jnp.zeros((bq, 128), f32)
            acc = jnp.zeros((bq, HS), f32)
        for n in range(TOK // ck):
            cols = pl.ds(n * ck, ck)
            if i_s is not None:
                sn = mm(qb, kh[cols, :], NT)
                s_write[:, cols] = sn
                for j in range(ck // 128):
                    top = jnp.maximum(top, sn[:, j * 128:(j + 1) * 128])
            if i_p is not None:
                p = jnp.exp2((s_read[:, cols] - peak) * scale2)
                for j in range(ck // 128):
                    l = l + p[:, j * 128:(j + 1) * 128]
                pb = p.astype(bf16)
                probs[r, cols] = pb
                acc = acc + mm(pb, vh[cols, :], NN)
        if i_p is not None:
            l_col = jnp.sum(l, axis=1, keepdims=True)
            inv = 1.0 / l_col
            oh[r, :] = (acc * inv).astype(bf16)
            inv_row = 1.0 / jnp.sum(jnp.transpose(l), axis=0, keepdims=True)
            wrow[:, r] = inv_row
            memberl[:, r] = (member[:, r].astype(f32) * inv_row).astype(bf16)
            qt = jnp.transpose(qh[r, :].astype(f32))
            qwt[:, r] = (qt * (inv_row * (1.0 / math.sqrt(HS)))).astype(bf16)
            mine = pl.ds(pl.multiple_of(g * HS, HS), HS)
            other = ch * 2 + (1 - c)
            same = ch * 2 + c
            remote(
                oh.at[rows(other, TD), :], lat_out.at[:, mine], sem_send.at[3], sem_recv.at[3], other
            ).start()

            @pl.when(ch != chip)
            def _():
                remote(
                    oh.at[rows(same, TD), :], lat_out.at[:, mine], sem_send.at[3], sem_recv.at[3], same
                ).start()

            @pl.when(ch == chip)
            def _():
                pltpu.make_async_copy(
                    oh.at[rows(same, TD), :], lat_out.at[:, mine], sem_recv.at[3]
                ).start()

        if i_s is not None:
            return jnp.max(top, axis=1, keepdims=True)

    drain(kh, sem_recv.at[0])
    peak0 = step(0, sa, None, None, None)
    drain(vh, sem_recv.at[1])

    @pl.loop(0, 7, init_carry=peak0)
    def fwd(i, peak):
        peak1 = step(2 * i + 1, sb, 2 * i, sa, peak)
        return step(2 * i + 2, sa, 2 * i + 1, sb, peak1)

    peak15 = step(15, sb, 14, sa, fwd)
    step(None, None, 15, sb, peak15)

    pooled = mm(member[...], oh[...], NN) * inv_count
    square = jnp.sum(pooled * pooled, axis=1, keepdims=True)
    pooled_b = pooled.astype(bf16)
    for n in range(DH // 512):
        cols = pl.ds(n * 512, 512)
        rs_src[:, cols] = mm(pooled_b, w_ref[:, cols], NN).astype(bf16)
    lane_o = lax.broadcasted_iota(jnp.int32, (FP, OT), 1)

    def high_low(value):
        high = value.astype(bf16).astype(f32)
        return jnp.where(lane_o == 0, high, jnp.where(lane_o == 1, value - high, 0.0))

    rs_src[:, DH:] = high_low(square).astype(bf16)
    owner = chip + 16 * c

    for off in FAR:
        p = peer(off)
        o = p // 2 + 16 * (p % 2)

        @pl.when(o < OWN)
        def _():
            remote(
                rs_src.at[:, rows(o, OT)], rs_recv.at[rows(g, FP), :],
                sem_send.at[4], sem_recv.at[4], p,
            ).start()

    @pl.when(owner < OWN)
    def _():
        pltpu.make_async_copy(
            rs_src.at[:, rows(owner, OT)], rs_recv.at[rows(g, FP), :], sem_recv.at[4]
        ).start()

    def frame_sums(lo, hi):
        for n in range(lo, hi):
            cols = pl.ds(n * 512, 512)
            rbuf[:, cols] = mm(memberl[...], probs[:, cols], NN).astype(bf16)

    frame_sums(0, 3)

    @pl.when(owner < OWN)
    def _():
        drain(rs_recv, sem_recv.at[4])
        total = jnp.zeros((FP, OT), f32)
        for n in range(GEN):
            total = total + rs_recv[n * FP:(n + 1) * FP, :].astype(f32)
        both = high_low(total[:, 0:1] + total[:, 1:2])
        total = jnp.where(owner == OWN - 1, both, total)
        ag_src[...] = total.astype(bf16)
        pltpu.make_async_copy(ag_src, proj.at[:, rows(owner, OT)], sem_recv.at[5]).start()
        for off in FAR:
            p = peer(off)
            remote(
                ag_src, proj.at[:, rows(owner, OT)], sem_send.at[5], sem_recv.at[5], p
            ).start()

    frame_sums(3, 8)
    pltpu.make_async_copy(rbuf.at[:, rows(g, TD)], r_all.at[rows(g, FP), :], sem_recv.at[6]).start()
    for off in FAR:
        p = peer(off)
        remote(
            rbuf.at[:, rows(p, TD)], r_all.at[rows(g, FP), :], sem_send.at[6], sem_recv.at[6], p
        ).start()
    drain(proj, sem_recv.at[5])

    squares = proj[:, DH:DH + 128].astype(f32)
    squares = squares[:, 0:1] + squares[:, 1:2]
    root = jnp.sqrt(squares / (GEN * HS) + EPS)
    score = jnp.zeros((FP, 1), f32)
    for n in range(DH // 512):
        cols = pl.ds(n * 512, 512)
        pre = proj[:, cols].astype(f32) / root
        feature = pre * jax.nn.sigmoid(pre)
        gsf[:, cols] = feature
        score = score + jnp.sum(feature * head_rows[:, cols], axis=1, keepdims=True)
    weight = (time_ref[0].astype(f32) + 1.0) / NSTEPS
    grad_score = -weight * jax.nn.sigmoid(-score) / FRAMES
    dot_sum = jnp.zeros((FP, 1), f32)
    grad_pooled = jnp.zeros((FP, HS), f32)
    for n in range(DH // 512):
        cols = pl.ds(n * 512, 512)
        pre = proj[:, cols].astype(f32) / root
        gate = jax.nn.sigmoid(pre)
        grad_pre = grad_score * head_rows[:, cols] * gate * (1.0 + pre * (1.0 - gate))
        dot_sum = dot_sum + jnp.sum(grad_pre * pre, axis=1, keepdims=True)
        grad_pooled = grad_pooled + mm((grad_pre / root).astype(bf16), w_ref[:, cols], NT)
    grad_root = -dot_sum / root
    grad_pooled = grad_pooled + (grad_root / root / (GEN * HS)) * pooled
    table = (TOK * (grad_pooled * inv_count)).astype(bf16)
    g_src[...] = table
    pltpu.make_async_copy(g_src, g_all.at[rows(g, FP), :], sem_recv.at[7]).start()
    for off in FAR:
        p = peer(off)
        remote(g_src, g_all.at[rows(g, FP), :], sem_send.at[7], sem_recv.at[7], p).start()

    for n in range(DH // 512):
        cols = pl.ds(n * 512, 512)
        value = grad_score * gsf[:, cols]
        high = value.astype(bf16)
        low = (value - high.astype(f32)).astype(bf16)
        hp_src[:, cols] = (mm(picked_t, high, NN) + mm(picked_t, low, NN)).astype(bf16)
    pltpu.make_async_copy(hp_src, hp_all.at[rows(x, 16), :], sem_recv.at[8]).start()
    for d in range(1, GRP):
        pltpu.make_async_remote_copy(
            src_ref=hp_src, dst_ref=hp_all.at[rows(x, 16), :],
            send_sem=sem_send.at[8], recv_sem=sem_recv.at[8],
            device_id={"grp": (x + d) % GRP}, device_id_type=MESH,
        ).start()

    bt = 512
    cb = 1024
    dkt[...] = jnp.zeros_like(dkt)
    mine = pl.ds(pl.multiple_of(g * HS, HS), HS)

    @pl.loop(0, TOK // bt)
    def _(i):
        blk = (i + g // 4) % (TOK // bt)
        r = rows(blk, bt)
        grad_rows = mm(member[:, r], g_src[...], TN)
        delta = jnp.sum(grad_rows * oh[r, :].astype(f32), axis=1, keepdims=True)
        grad_b = grad_rows.astype(bf16)
        acc = jnp.zeros((bt, HS), f32)
        qb = qwt[:, r]
        for n in range(TOK // cb):
            cols = pl.ds(n * cb, cb)
            dp = mm(grad_b, vh[cols, :], NT)
            ds = (dp - delta).astype(bf16) * probs[r, cols]
            acc = acc + mm(ds, kh[cols, :], NN)
            dkt[:, cols] += mm(qb, ds, NN)
        w_cols = jnp.transpose(jnp.broadcast_to(wrow[:, r] * (1.0 / math.sqrt(HS)), (HS, bt)))
        qh[r, :] = (acc * w_cols).astype(bf16)
        for d in range(bt // TD):
            p = blk * (bt // TD) + d

            @pl.when(p != g)
            def _():
                remote(
                    qh.at[rows(p, TD), :], dq_out.at[:, mine], sem_send.at[9], sem_recv.at[9], p
                ).start()

            @pl.when(p == g)
            def _():
                pltpu.make_async_copy(
                    qh.at[rows(p, TD), :], dq_out.at[:, mine], sem_recv.at[9]
                ).start()

    for off in FAR + [None]:
        p = g if off is None else peer(off)
        kh[rows(p, TD), :] = jnp.transpose(dkt[:, rows(p, TD)]).astype(bf16)
        if off is None:
            pltpu.make_async_copy(kh.at[rows(p, TD), :], dk_out.at[:, mine], sem_recv.at[10]).start()
        else:
            remote(
                kh.at[rows(p, TD), :], dk_out.at[:, mine], sem_send.at[10], sem_recv.at[10], p
            ).start()

    drain(r_all, sem_recv.at[6])
    drain(g_all, sem_recv.at[7])
    for h in range(GEN):
        hr = pl.ds(h * FP, FP)
        dv_out[:, h * HS:(h + 1) * HS] = mm(r_all[hr, :], g_all[hr, :], TN).astype(bf16)
    drain(hp_all, sem_recv.at[8])
    total = jnp.zeros((16, DH), f32)
    for n in range(GRP):
        total = total + hp_all[n * 16:(n + 1) * 16, :].astype(f32)
    gh_out[...] = total[:NDH, :]

    drain(lat_out, sem_recv.at[3])
    drain(dq_out, sem_recv.at[9])
    drain(dk_out, sem_recv.at[10])
    sent = kh.at[pl.ds(0, (GEN - 1) * TD), :]
    for n in (0, 1, 2, 3, 9, 10):
        drain(sent, sem_send.at[n])

    @pl.when(owner < OWN)
    def _():
        drain(rs_src.at[:, pl.ds(0, (OWN - 1) * OT)], sem_send.at[4])
        drain(rs_recv.at[pl.ds(0, (GEN - 1) * FP), :], sem_send.at[5])

    @pl.when(owner >= OWN)
    def _():
        drain(rs_src, sem_send.at[4])

    drain(r_all.at[pl.ds(0, (GEN - 1) * FP), :], sem_send.at[6])
    drain(g_all.at[pl.ds(0, (GEN - 1) * FP), :], sem_send.at[7])
    drain(hp_all.at[pl.ds(0, (GRP - 1) * 16), :], sem_send.at[8])


def on_device(
    query_in, key_in, value_in, teacher_w, disc_heads, frame_of_token, head_of_frame, timestep
):
    vmem = pl.BlockSpec(memory_space=pltpu.VMEM)
    smem = pl.BlockSpec(memory_space=pltpu.SMEM)
    hbm = pl.BlockSpec(memory_space=pl.ANY)
    rows_shape = jax.ShapeDtypeStruct((TD, GEN * HS), bf16)
    V = pltpu.VMEM
    outs = pl.pallas_call(
        body,
        out_shape=(
            rows_shape, rows_shape, rows_shape, rows_shape,
            jax.ShapeDtypeStruct((NDH, DH), f32),
        ),
        in_specs=[hbm, hbm, hbm, vmem, vmem, vmem, smem, smem],
        out_specs=(hbm, hbm, hbm, vmem, vmem),
        scratch_shapes=[
            V((TOK, TOK), bf16),
            V((TOK, HS), bf16), V((TOK, HS), bf16), V((TOK, HS), bf16), V((TOK, HS), bf16),
            V((256, TOK), f32), V((256, TOK), f32),
            V((HS, TOK), f32), V((HS, TOK), bf16), V((1, TOK), f32),
            V((FP, TOK), bf16), V((FP, TOK), bf16), V((FP, TOK), bf16),
            V((GEN * FP, TD), bf16), V((FP, HS), bf16), V((GEN * FP, HS), bf16),
            V((FP, DH + OT), bf16), V((GEN * FP, OT), bf16), V((FP, OT), bf16),
            V((FP, DH + OT), bf16), V((FP, DH), f32), V((FP, DH), f32),
            V((16, DH), bf16), V((GRP * 16, DH), bf16),
            pltpu.SemaphoreType.DMA((11,)),
            pltpu.SemaphoreType.DMA((16,)),
            pltpu.SemaphoreType.DMA((11,)),
        ],
        compiler_params=pltpu.CompilerParams(
            collective_id=0, has_side_effects=True, vmem_limit_bytes=63 * 1024 * 1024
        ),
        name="clip_step",
    )(
        query_in[0], key_in[0], value_in[0], teacher_w, disc_heads,
        frame_of_token, head_of_frame, timestep,
    )
    lat, dq, dk, dv, gh = outs
    return (lat[None], dq[None], dk[None], dv[None], gh)


def solution(mesh):
    return jax.shard_map(
        on_device,
        mesh=mesh,
        in_specs=(
            P("grp", "gen", None),
            P("grp", "gen", None),
            P("grp", "gen", None),
            P("gen", None),
            P(),
            P("grp", None),
            P("grp", None),
            P("grp"),
        ),
        out_specs=(
            P("grp", "gen", None),
            P("grp", "gen", None),
            P("grp", "gen", None),
            P("grp", "gen", None),
            P(),
        ),
        check_vma=False,
    )
```

```python
import functools
import math

import jax
import jax.numpy as jnp
from jax import lax
from jax.experimental import pallas as pl
from jax.experimental.pallas import tpu as pltpu
from jax.sharding import PartitionSpec as P

HS = 128
FRAMES = 21
NDH = 8
NSTEPS = 1000
EPS = 1e-06
GEN = 32
GRP = 4
TOK = 4096
TD = 128
DH = 5120
FP = 32
OT = 256
OWN = 21
MESH = pl.DeviceIdType.MESH
f32 = jnp.float32
bf16 = jnp.bfloat16
NT = (((1,), (1,)), ((), ()))
NN = (((1,), (0,)), ((), ()))
TN = (((0,), (0,)), ((), ()))
CHIPS = [
    (2, 2), (3, 2), (2, 3), (1, 2), (2, 1), (0, 2), (2, 0), (3, 1), (1, 3), (3, 3), (1, 1),
    (0, 3), (0, 1), (3, 0), (1, 0),
]
FAR = [(dy, dz, dc) for dy, dz in CHIPS for dc in (0, 1)] + [(0, 0, 1)]


def mm(a, b, dims):
    return lax.dot_general(a, b, dims, preferred_element_type=f32)


def body(
    q_in, k_in, v_in, w_ref, disc_ref, frames_ref, hof_ref, time_ref,
    lat_out, dq_out, dk_out, dv_out, gh_out,
    probs, qh, kh, vh, oh, sa, sb, dkt, qwt, wrow, member, memberl, rbuf, r_all, g_src, g_all,
    rs_src, rs_recv, ag_src, proj, head_rows, gsf, hp_src, hp_all, dob,
    sem_send, sem_q, sem_recv,
):
    g = lax.axis_index("gen")
    x = lax.axis_index("grp")
    y = g // 8
    z = (g // 2) % 4
    c = g % 2
    chip = g // 2

    def peer(off):
        dy, dz, dc = off
        ey = dy + c * (dz - dy)
        ez = dz + c * (dy - dz)
        return ((y + ey) % 4) * 8 + ((z + ez) % 4) * 2 + (c + dc) % 2

    def rows(i, n):
        return pl.ds(pl.multiple_of(i * n, n), n)

    def remote(src, dst, send, recv, dev):
        return pltpu.make_async_remote_copy(
            src_ref=src, dst_ref=dst, send_sem=send, recv_sem=recv,
            device_id={"gen": dev}, device_id_type=MESH,
        )

    def drain(ref, sem):
        pltpu.make_async_copy(ref, ref, sem).wait()

    barrier = pltpu.get_barrier_semaphore()
    for off in FAR:
        pl.semaphore_signal(barrier, inc=1, device_id={"gen": peer(off)}, device_id_type=MESH)
    for d in range(1, GRP):
        pl.semaphore_signal(
            barrier, inc=1, device_id={"grp": (x + d) % GRP}, device_id_type=MESH
        )
    pl.semaphore_wait(barrier, GEN - 1 + GRP - 1)

    for src, dst, which in ((k_in, kh, 0), (v_in, vh, 1)):
        pltpu.make_async_copy(src.at[:, rows(g, TD)], dst.at[rows(g, TD), :], sem_recv.at[which]).start()
        for off in FAR:
            p = peer(off)
            remote(
                src.at[:, rows(p, TD)], dst.at[rows(g, TD), :],
                sem_send.at[which], sem_recv.at[which], p,
            ).start()

    def q_chip(i, sign):
        dy = i % 4
        dz = (i // 4 + i) % 4
        return ((y + sign * dy + 4) % 4) * 4 + (z + sign * dz + 4) % 4

    pltpu.make_async_copy(q_in.at[:, rows(g, TD)], qh.at[rows(g, TD), :], sem_q.at[0]).start()
    for i in range(16):
        for dc in (0, 1):
            if i == 0 and dc == 0:
                continue
            p = q_chip(i, 1) * 2 + (c + dc) % 2
            remote(
                q_in.at[:, rows(p, TD)], qh.at[rows(g, TD), :], sem_send.at[2], sem_q.at[i], p
            ).start()

    frames = frames_ref[...]
    mem = (frames == lax.broadcasted_iota(jnp.int32, (FP, TOK), 0)).astype(f32)
    member[...] = mem.astype(bf16)
    counts = jnp.sum(mem, axis=1, keepdims=True)
    inv_count = jnp.where(counts > 0.0, 1.0 / jnp.maximum(counts, 1.0), 0.0)
    lane_n = lax.broadcasted_iota(jnp.int32, (FP, 128), 1)
    sub_n = lax.broadcasted_iota(jnp.int32, (FP, 128), 0)
    lane_8 = lax.broadcasted_iota(jnp.int32, (16, 128), 1)
    sub_8 = lax.broadcasted_iota(jnp.int32, (16, 128), 0)
    picked = jnp.zeros((FP, 128), f32)
    picked_t = jnp.zeros((16, 128), f32)
    for f in range(FRAMES):
        j = hof_ref[0, f]
        picked = jnp.where((sub_n == f) & (lane_n == j), 1.0, picked)
        picked_t = jnp.where((lane_8 == f) & (sub_8 == j), 1.0, picked_t)
    picked = picked[:, :NDH].astype(bf16)
    picked_t = picked_t[:, :FP].astype(bf16)
    for n in range(DH // 512):
        cols = pl.ds(n * 512, 512)
        part = disc_ref[:, cols]
        total = jnp.zeros((FP, 512), f32)
        for _ in range(3):
            high = part.astype(bf16)
            total = total + mm(picked, high, NN)
            part = part - high.astype(f32)
        head_rows[:, cols] = total

    scale2 = math.log2(math.e) / math.sqrt(HS)
    ck = 512
    bq = 256

    def step(i_s, s_write, i_p, s_read, peak):
        if i_s is not None:
            drain(qh.at[pl.ds(0, bq), :], sem_q.at[i_s])
            qb = qh[rows(q_chip(i_s, -1), bq), :]
            top = jnp.full((bq, 128), -jnp.inf, f32)
            qwt[:, rows(q_chip(i_s, -1), bq)] = jnp.transpose(qb.astype(f32)).astype(bf16)
        if i_p is not None:
            ch = q_chip(i_p, -1)
            r = rows(ch, bq)
            l = jnp.zeros((bq, 128), f32)
            acc = jnp.zeros((bq, HS), f32)
        for n in range(TOK // ck):
            cols = pl.ds(n * ck, ck)
            if i_s is not None:
                sn = mm(qb, kh[cols, :], NT)
                s_write[:, cols] = sn
                for j in range(ck // 128):
                    top = jnp.maximum(top, sn[:, j * 128:(j + 1) * 128])
            if i_p is not None:
                p = jnp.exp2((s_read[:, cols] - peak) * scale2)
                for j in range(ck // 128):
                    l = l + p[:, j * 128:(j + 1) * 128]
                pb = p.astype(bf16)
                probs[r, cols] = pb
                acc = acc + mm(pb, vh[cols, :], NN)
        if i_p is not None:
            l_col = jnp.sum(l, axis=1, keepdims=True)
            inv = 1.0 / l_col
            oh[r, :] = (acc * inv).astype(bf16)
            wrow[:, r] = 1.0 / jnp.sum(jnp.transpose(l), axis=0, keepdims=True)
            mine = pl.ds(pl.multiple_of(g * HS, HS), HS)
            other = ch * 2 + (1 - c)
            same = ch * 2 + c
            remote(
                oh.at[rows(other, TD), :], lat_out.at[:, mine], sem_send.at[3], sem_recv.at[3], other
            ).start()

            @pl.when(ch != chip)
            def _():
                remote(
                    oh.at[rows(same, TD), :], lat_out.at[:, mine], sem_send.at[3], sem_recv.at[3], same
                ).start()

            @pl.when(ch == chip)
            def _():
                pltpu.make_async_copy(
                    oh.at[rows(same, TD), :], lat_out.at[:, mine], sem_recv.at[3]
                ).start()

        if i_s is not None:
            return jnp.max(top, axis=1, keepdims=True)

    drain(kh, sem_recv.at[0])
    peak0 = step(0, sa, None, None, None)
    drain(vh, sem_recv.at[1])

    @pl.loop(0, 7, init_carry=peak0)
    def fwd(i, peak):
        peak1 = step(2 * i + 1, sb, 2 * i, sa, peak)
        return step(2 * i + 2, sa, 2 * i + 1, sb, peak1)

    peak15 = step(15, sb, 14, sa, fwd)
    step(None, None, 15, sb, peak15)

    pooled = mm(member[...], oh[...], NN) * inv_count
    square = jnp.sum(pooled * pooled, axis=1, keepdims=True)
    pooled_b = pooled.astype(bf16)
    for n in range(DH // 512):
        cols = pl.ds(n * 512, 512)
        rs_src[:, cols] = mm(pooled_b, w_ref[:, cols], NN).astype(bf16)
    lane_o = lax.broadcasted_iota(jnp.int32, (FP, OT), 1)

    def high_low(value):
        high = value.astype(bf16).astype(f32)
        return jnp.where(lane_o == 0, high, jnp.where(lane_o == 1, value - high, 0.0))

    rs_src[:, DH:] = high_low(square).astype(bf16)
    owner = chip + 16 * c

    for off in FAR:
        p = peer(off)
        o = p // 2 + 16 * (p % 2)

        @pl.when(o < OWN)
        def _():
            remote(
                rs_src.at[:, rows(o, OT)], rs_recv.at[rows(g, FP), :],
                sem_send.at[4], sem_recv.at[4], p,
            ).start()

    @pl.when(owner < OWN)
    def _():
        pltpu.make_async_copy(
            rs_src.at[:, rows(owner, OT)], rs_recv.at[rows(g, FP), :], sem_recv.at[4]
        ).start()

    def frame_sums(lo, hi):
        for n in range(lo, hi):
            cols = pl.ds(n * 512, 512)
            rbuf[:, cols] = mm(memberl[...], probs[:, cols], NN).astype(bf16)

    memberl[...] = (member[...].astype(f32) * wrow[...]).astype(bf16)
    frame_sums(0, 4)

    @pl.when(owner < OWN)
    def _():
        drain(rs_recv, sem_recv.at[4])
        total = jnp.zeros((FP, OT), f32)
        for n in range(GEN):
            total = total + rs_recv[n * FP:(n + 1) * FP, :].astype(f32)
        both = high_low(total[:, 0:1] + total[:, 1:2])
        total = jnp.where(owner == OWN - 1, both, total)
        ag_src[...] = total.astype(bf16)
        pltpu.make_async_copy(ag_src, proj.at[:, rows(owner, OT)], sem_recv.at[5]).start()
        for off in FAR:
            p = peer(off)
            remote(
                ag_src, proj.at[:, rows(owner, OT)], sem_send.at[5], sem_recv.at[5], p
            ).start()

    frame_sums(4, 8)
    pltpu.make_async_copy(rbuf.at[:, rows(g, TD)], r_all.at[rows(g, FP), :], sem_recv.at[6]).start()
    for off in FAR:
        p = peer(off)
        remote(
            rbuf.at[:, rows(p, TD)], r_all.at[rows(g, FP), :], sem_send.at[6], sem_recv.at[6], p
        ).start()
    drain(proj, sem_recv.at[5])

    squares = proj[:, DH:DH + 128].astype(f32)
    squares = squares[:, 0:1] + squares[:, 1:2]
    root = jnp.sqrt(squares / (GEN * HS) + EPS)
    inv_root = 1.0 / root
    score = jnp.zeros((FP, 1), f32)
    dot_sum = jnp.zeros((FP, 1), f32)
    raw = jnp.zeros((FP, HS), f32)
    for n in range(DH // 512):
        cols = pl.ds(n * 512, 512)
        hr = head_rows[:, cols]
        pre = proj[:, cols].astype(f32) * inv_root
        gate = jax.nn.sigmoid(pre)
        feature = pre * gate
        gsf[:, cols] = feature
        slope = hr * (gate + feature * (1.0 - gate))
        score = score + jnp.sum(feature * hr, axis=1, keepdims=True)
        dot_sum = dot_sum + jnp.sum(slope * pre, axis=1, keepdims=True)
        raw = raw + mm(slope.astype(bf16), w_ref[:, cols], NT)
    weight = (time_ref[0].astype(f32) + 1.0) / NSTEPS
    grad_score = -weight * jax.nn.sigmoid(-score) / FRAMES
    grad_pooled = (grad_score * inv_root) * raw
    grad_pooled = grad_pooled - (grad_score * dot_sum * inv_root * inv_root / (GEN * HS)) * pooled
    table = (TOK * (grad_pooled * inv_count)).astype(bf16)
    g_src[...] = table
    pltpu.make_async_copy(g_src, g_all.at[rows(g, FP), :], sem_recv.at[7]).start()
    for off in FAR:
        p = peer(off)
        remote(g_src, g_all.at[rows(g, FP), :], sem_send.at[7], sem_recv.at[7], p).start()

    bt = 512
    half = TOK // bt // 2
    cb = 1024
    inv_scale = 1.0 / math.sqrt(HS)
    mine = pl.ds(pl.multiple_of(g * HS, HS), HS)
    spin = g // 4

    def give(src, p, out, which):
        @pl.when(p != g)
        def _():
            remote(
                src.at[rows(p, TD), :], out.at[:, mine], sem_send.at[which], sem_recv.at[which], p
            ).start()

        @pl.when(p == g)
        def _():
            pltpu.make_async_copy(
                src.at[rows(p, TD), :], out.at[:, mine], sem_recv.at[which]
            ).start()

    def block_of(i):
        return (i + spin) % (TOK // bt)

    def grads_of(r):
        grad_rows = mm(member[:, r], g_src[...], TN)
        delta = jnp.sum(grad_rows * oh[r, :].astype(f32), axis=1, keepdims=True)
        return grad_rows.astype(bf16), delta

    def scaled_q(r):
        return (qwt[:, r].astype(f32) * (wrow[:, r] * inv_scale)).astype(bf16)

    def finish_q(r, acc):
        w_cols = jnp.transpose(jnp.broadcast_to(wrow[:, r] * inv_scale, (HS, bt)))
        qh[r, :] = (acc * w_cols).astype(bf16)

    def part(j, k):
        return pl.ds((2 * j + k) * HS, HS)

    def store_part(ref, j, value):
        ref[:, part(j, 0)] = value[:bq, :]
        ref[:, part(j, 1)] = value[bq:, :]

    def load_part(ref, j):
        return jnp.concatenate([ref[:, part(j, 0)], ref[:, part(j, 1)]], axis=0)

    dkt[...] = jnp.zeros_like(dkt)

    @pl.loop(0, half)
    def _(i):
        blk = block_of(i)
        r = rows(blk, bt)
        grad_b, delta = grads_of(r)
        acc = jnp.zeros((bt, HS), f32)
        qb = scaled_q(r)
        for n in range(TOK // cb):
            cols = pl.ds(n * cb, cb)
            dp = mm(grad_b, vh[cols, :], NT)
            ds = (dp - delta).astype(bf16) * probs[r, cols]
            acc = acc + mm(ds, kh[cols, :], NN)
            dkt[:, cols] += mm(qb, ds, NN)
        finish_q(r, acc)
        for d in range(bt // TD):
            give(qh, blk * (bt // TD) + d, dq_out, 9)

    for j in range(half):
        r = rows(block_of(half + j), bt)
        grad_b, delta = grads_of(r)
        dob[j * bt:(j + 1) * bt, :] = grad_b
        store_part(sb, j, jnp.broadcast_to(delta, (bt, HS)))
        store_part(sa, j, jnp.zeros((bt, HS), f32))
        qwt[:, r] = scaled_q(r)

    @pl.loop(0, TOK // bt)
    def _(i):
        blk = block_of(i)
        cols = rows(blk, bt)
        kc = kh[cols, :]
        vc = vh[cols, :]
        dk = dkt[:, cols]
        for j in range(half):
            r = rows(block_of(half + j), bt)
            jr = slice(j * bt, (j + 1) * bt)
            dp = mm(dob[jr, :], vc, NT)
            ds = (dp - load_part(sb, j)[:, 0:1]).astype(bf16) * probs[r, cols]
            store_part(sa, j, load_part(sa, j) + mm(ds, kc, NN))
            dk = dk + mm(qwt[:, r], ds, NN)
        kh[cols, :] = jnp.transpose(dk).astype(bf16)
        for d in range(bt // TD):
            give(kh, blk * (bt // TD) + d, dk_out, 10)

    for j in range(half):
        blk = block_of(half + j)
        finish_q(rows(blk, bt), load_part(sa, j))
        for d in range(bt // TD):
            give(qh, blk * (bt // TD) + d, dq_out, 9)

    for n in range(DH // 512):
        cols = pl.ds(n * 512, 512)
        value = grad_score * gsf[:, cols]
        high = value.astype(bf16)
        low = (value - high.astype(f32)).astype(bf16)
        hp_src[:, cols] = (mm(picked_t, high, NN) + mm(picked_t, low, NN)).astype(bf16)
    pltpu.make_async_copy(hp_src, hp_all.at[rows(x, 16), :], sem_recv.at[8]).start()
    for d in range(1, GRP):
        pltpu.make_async_remote_copy(
            src_ref=hp_src, dst_ref=hp_all.at[rows(x, 16), :],
            send_sem=sem_send.at[8], recv_sem=sem_recv.at[8],
            device_id={"grp": (x + d) % GRP}, device_id_type=MESH,
        ).start()

    drain(r_all, sem_recv.at[6])
    drain(g_all, sem_recv.at[7])
    for h in range(GEN):
        hr = pl.ds(h * FP, FP)
        qwt[:, h * HS:(h + 1) * HS] = mm(r_all[hr, :], g_all[hr, :], TN).astype(bf16)
    to_dv = pltpu.make_async_copy(qwt, dv_out, sem_recv.at[1])
    to_dv.start()
    drain(hp_all, sem_recv.at[8])
    total = jnp.zeros((16, DH), f32)
    for n in range(GRP):
        total = total + hp_all[n * 16:(n + 1) * 16, :].astype(f32)
    gh_out[...] = total[:NDH, :]

    to_dv.wait()
    drain(lat_out, sem_recv.at[3])
    drain(dq_out, sem_recv.at[9])
    drain(dk_out, sem_recv.at[10])
    sent = kh.at[pl.ds(0, (GEN - 1) * TD), :]
    for n in (0, 1, 2, 3, 9, 10):
        drain(sent, sem_send.at[n])

    @pl.when(owner < OWN)
    def _():
        drain(rs_src.at[:, pl.ds(0, (OWN - 1) * OT)], sem_send.at[4])
        drain(rs_recv.at[pl.ds(0, (GEN - 1) * FP), :], sem_send.at[5])

    @pl.when(owner >= OWN)
    def _():
        drain(rs_src, sem_send.at[4])

    drain(r_all.at[pl.ds(0, (GEN - 1) * FP), :], sem_send.at[6])
    drain(g_all.at[pl.ds(0, (GEN - 1) * FP), :], sem_send.at[7])
    drain(hp_all.at[pl.ds(0, (GRP - 1) * 16), :], sem_send.at[8])


def settle(*refs):
    sem = refs[-1]
    n = (len(refs) - 1) // 2
    copies = []
    for i in range(n):
        parts = 4 if i < n - 1 else 1
        step = refs[i].shape[0] // parts
        for j in range(parts):
            r = pl.ds(j * step, step)
            copy = pltpu.make_async_copy(refs[i].at[r], refs[n + i].at[r], sem.at[len(copies)])
            copy.start()
            copies.append(copy)
    for copy in copies:
        copy.wait()


def on_device(
    query_in, key_in, value_in, teacher_w, disc_heads, frame_of_token, head_of_frame, timestep
):
    vmem = pl.BlockSpec(memory_space=pltpu.VMEM)
    smem = pl.BlockSpec(memory_space=pltpu.SMEM)
    hbm = pl.BlockSpec(memory_space=pl.ANY)
    rows_shape = jax.ShapeDtypeStruct((TD, GEN * HS), bf16)
    V = pltpu.VMEM
    outs = pl.pallas_call(
        body,
        out_shape=(
            rows_shape, rows_shape, rows_shape, rows_shape,
            jax.ShapeDtypeStruct((NDH, DH), f32),
        ),
        in_specs=[hbm, hbm, hbm, vmem, vmem, vmem, smem, smem],
        out_specs=(hbm, hbm, hbm, hbm, vmem),
        scratch_shapes=[
            V((TOK, TOK), bf16),
            V((TOK, HS), bf16), V((TOK, HS), bf16), V((TOK, HS), bf16), V((TOK, HS), bf16),
            V((256, TOK), f32), V((256, TOK), f32),
            V((HS, TOK), f32), V((HS, TOK), bf16), V((1, TOK), f32),
            V((FP, TOK), bf16), V((FP, TOK), bf16), V((FP, TOK), bf16),
            V((GEN * FP, TD), bf16), V((FP, HS), bf16), V((GEN * FP, HS), bf16),
            V((FP, DH + OT), bf16), V((GEN * FP, OT), bf16), V((FP, OT), bf16),
            V((FP, DH + OT), bf16), V((FP, DH), f32), V((FP, DH), f32),
            V((16, DH), bf16), V((GRP * 16, DH), bf16),
            V((TOK // 2, HS), bf16),
            pltpu.SemaphoreType.DMA((11,)),
            pltpu.SemaphoreType.DMA((16,)),
            pltpu.SemaphoreType.DMA((11,)),
        ],
        compiler_params=pltpu.CompilerParams(
            collective_id=0, has_side_effects=True, vmem_limit_bytes=63 * 1024 * 1024
        ),
        name="clip_step",
    )(
        query_in[0], key_in[0], value_in[0], teacher_w, disc_heads,
        frame_of_token, head_of_frame, timestep,
    )
    lat, dq, dk, dv, gh = pl.pallas_call(
        settle,
        out_shape=tuple(jax.ShapeDtypeStruct(o.shape, o.dtype) for o in outs),
        in_specs=[hbm] * 5,
        out_specs=(hbm,) * 5,
        scratch_shapes=[pltpu.SemaphoreType.DMA((17,))],
        name="settle",
    )(*outs)
    return (lat[None], dq[None], dk[None], dv[None], gh)


def solution(mesh):
    return jax.shard_map(
        on_device,
        mesh=mesh,
        in_specs=(
            P("grp", "gen", None),
            P("grp", "gen", None),
            P("grp", "gen", None),
            P("gen", None),
            P(),
            P("grp", None),
            P("grp", None),
            P("grp"),
        ),
        out_specs=(
            P("grp", "gen", None),
            P("grp", "gen", None),
            P("grp", "gen", None),
            P("grp", "gen", None),
            P(),
        ),
        check_vma=False,
    )
```

```python
import functools
import math

import jax
import jax.numpy as jnp
from jax import lax
from jax.experimental import pallas as pl
from jax.experimental.pallas import tpu as pltpu
from jax.sharding import PartitionSpec as P

HS = 128
FRAMES = 21
NDH = 8
NSTEPS = 1000
EPS = 1e-06
GEN = 32
GRP = 4
TOK = 4096
TD = 128
DH = 5120
FP = 32
OT = 256
OWN = 21
MESH = pl.DeviceIdType.MESH
f32 = jnp.float32
bf16 = jnp.bfloat16
NT = (((1,), (1,)), ((), ()))
NN = (((1,), (0,)), ((), ()))
TN = (((0,), (0,)), ((), ()))
CHIPS = [
    (2, 2), (3, 2), (2, 3), (1, 2), (2, 1), (0, 2), (2, 0), (3, 1), (1, 3), (3, 3), (1, 1),
    (0, 3), (0, 1), (3, 0), (1, 0),
]
FAR = [(dy, dz, dc) for dy, dz in CHIPS for dc in (0, 1)] + [(0, 0, 1)]


def mm(a, b, dims):
    return lax.dot_general(a, b, dims, preferred_element_type=f32)


def body(
    q_in, k_in, v_in, w_ref, disc_ref, frames_ref, hof_ref, time_ref,
    lat_out, dq_out, dk_out, dv_out, gh_out,
    probs, qh, kh, vh, oh, sa, sb, dkt, qwt, wrow, member, memberl, rbuf, r_all, g_src, g_all,
    rs_src, rs_recv, ag_src, proj, head_rows, gsf, hp_src, hp_all,
    sem_send, sem_q, sem_recv,
):
    g = lax.axis_index("gen")
    x = lax.axis_index("grp")
    y = g // 8
    z = (g // 2) % 4
    c = g % 2
    chip = g // 2

    def peer(off):
        dy, dz, dc = off
        ey = dy + c * (dz - dy)
        ez = dz + c * (dy - dz)
        return ((y + ey) % 4) * 8 + ((z + ez) % 4) * 2 + (c + dc) % 2

    def rows(i, n):
        return pl.ds(pl.multiple_of(i * n, n), n)

    def remote(src, dst, send, recv, dev):
        return pltpu.make_async_remote_copy(
            src_ref=src, dst_ref=dst, send_sem=send, recv_sem=recv,
            device_id={"gen": dev}, device_id_type=MESH,
        )

    def drain(ref, sem):
        pltpu.make_async_copy(ref, ref, sem).wait()

    barrier = pltpu.get_barrier_semaphore()
    for off in FAR:
        pl.semaphore_signal(barrier, inc=1, device_id={"gen": peer(off)}, device_id_type=MESH)
    for d in range(1, GRP):
        pl.semaphore_signal(
            barrier, inc=1, device_id={"grp": (x + d) % GRP}, device_id_type=MESH
        )
    pl.semaphore_wait(barrier, GEN - 1 + GRP - 1)

    def q_chip(i, sign):
        dy = i % 4
        dz = (i // 4 + i) % 4
        return ((y + sign * dy + 4) % 4) * 4 + (z + sign * dz + 4) % 4

    def gather_rows(src, dst, which):
        pltpu.make_async_copy(
            src.at[:, rows(g, TD)], dst.at[rows(g, TD), :], sem_recv.at[which]
        ).start()
        for off in FAR:
            p = peer(off)
            remote(
                src.at[:, rows(p, TD)], dst.at[rows(g, TD), :],
                sem_send.at[which], sem_recv.at[which], p,
            ).start()

    gather_rows(k_in, kh, 0)
    pltpu.make_async_copy(q_in.at[:, rows(g, TD)], qh.at[rows(g, TD), :], sem_q.at[0]).start()
    for i in range(16):
        for dc in (0, 1):
            if i == 0 and dc == 0:
                continue
            p = q_chip(i, 1) * 2 + (c + dc) % 2
            remote(
                q_in.at[:, rows(p, TD)], qh.at[rows(g, TD), :], sem_send.at[2], sem_q.at[i], p
            ).start()
    gather_rows(v_in, vh, 1)

    frames = frames_ref[...]
    mem = (frames == lax.broadcasted_iota(jnp.int32, (FP, TOK), 0)).astype(f32)
    member[...] = mem.astype(bf16)
    counts = jnp.sum(mem, axis=1, keepdims=True)
    inv_count = jnp.where(counts > 0.0, 1.0 / jnp.maximum(counts, 1.0), 0.0)
    lane_n = lax.broadcasted_iota(jnp.int32, (FP, 128), 1)
    sub_n = lax.broadcasted_iota(jnp.int32, (FP, 128), 0)
    lane_8 = lax.broadcasted_iota(jnp.int32, (16, 128), 1)
    sub_8 = lax.broadcasted_iota(jnp.int32, (16, 128), 0)
    picked = jnp.zeros((FP, 128), f32)
    picked_t = jnp.zeros((16, 128), f32)
    for f in range(FRAMES):
        j = hof_ref[0, f]
        picked = jnp.where((sub_n == f) & (lane_n == j), 1.0, picked)
        picked_t = jnp.where((lane_8 == f) & (sub_8 == j), 1.0, picked_t)
    picked = picked[:, :NDH].astype(bf16)
    picked_t = picked_t[:, :FP].astype(bf16)
    for n in range(DH // 512):
        cols = pl.ds(n * 512, 512)
        part = disc_ref[:, cols]
        total = jnp.zeros((FP, 512), f32)
        for _ in range(3):
            high = part.astype(bf16)
            total = total + mm(picked, high, NN)
            part = part - high.astype(f32)
        head_rows[:, cols] = total

    scale2 = math.log2(math.e) / math.sqrt(HS)
    ck = 512
    bq = 256

    def step(i_s, s_write, i_p, s_read, peak):
        if i_s is not None:
            drain(qh.at[pl.ds(0, bq), :], sem_q.at[i_s])
            rs = rows(q_chip(i_s, -1), bq)
            qb = qh[rs, :]
            top = jnp.full((bq, 128), -jnp.inf, f32)
            qwt[:, rs] = jnp.transpose(qb.astype(f32)).astype(bf16)
        if i_p is not None:
            r = rows(q_chip(i_p, -1), bq)
            l = jnp.zeros((bq, 128), f32)
        for n in range(TOK // ck):
            cols = pl.ds(n * ck, ck)
            if i_s is not None:
                sn = mm(qb, kh[cols, :], NT)
                s_write[:, cols] = sn
                for j in range(ck // 128):
                    top = jnp.maximum(top, sn[:, j * 128:(j + 1) * 128])
            if i_p is not None:
                p = jnp.exp2((s_read[:, cols] - peak) * scale2)
                for j in range(ck // 128):
                    l = l + p[:, j * 128:(j + 1) * 128]
                probs[r, cols] = p.astype(bf16)
        if i_p is not None:
            wrow[:, r] = 1.0 / jnp.sum(jnp.transpose(l), axis=0, keepdims=True)
        if i_s is not None:
            return jnp.max(top, axis=1, keepdims=True)

    drain(kh, sem_recv.at[0])
    peak0 = step(0, sa, None, None, None)

    @pl.loop(0, 7, init_carry=peak0)
    def fwd(i, peak):
        peak1 = step(2 * i + 1, sb, 2 * i, sa, peak)
        return step(2 * i + 2, sa, 2 * i + 1, sb, peak1)

    peak15 = step(15, sb, 14, sa, fwd)
    step(None, None, 15, sb, peak15)

    bt = 512
    inv_scale = 1.0 / math.sqrt(HS)
    mine = pl.ds(pl.multiple_of(g * HS, HS), HS)

    def pair(i):
        return rows(q_chip(2 * i, -1), bq), rows(q_chip(2 * i + 1, -1), bq)

    def load_rows(ref, i, cols=slice(None)):
        r0, r1 = pair(i)
        return jnp.concatenate([ref[r0, cols], ref[r1, cols]], axis=0)

    def load_cols(ref, i):
        r0, r1 = pair(i)
        return jnp.concatenate([ref[:, r0], ref[:, r1]], axis=1)

    def store_rows(ref, i, value):
        r0, r1 = pair(i)
        ref[r0, :] = value[:bq]
        ref[r1, :] = value[bq:]

    def row_factor(i, factor):
        return jnp.transpose(jnp.broadcast_to(load_cols(wrow, i) * factor, (HS, bt)))

    def give(src, ch, out, which):
        other = ch * 2 + (1 - c)
        same = ch * 2 + c
        remote(
            src.at[rows(other, TD), :], out.at[:, mine], sem_send.at[which], sem_recv.at[which], other
        ).start()

        @pl.when(ch != chip)
        def _():
            remote(
                src.at[rows(same, TD), :], out.at[:, mine], sem_send.at[which], sem_recv.at[which], same
            ).start()

        @pl.when(ch == chip)
        def _():
            pltpu.make_async_copy(
                src.at[rows(same, TD), :], out.at[:, mine], sem_recv.at[which]
            ).start()

    def give_pair(src, i, out, which):
        give(src, q_chip(2 * i, -1), out, which)
        give(src, q_chip(2 * i + 1, -1), out, which)

    memberl[...] = (member[...].astype(f32) * wrow[...]).astype(bf16)
    drain(vh, sem_recv.at[1])

    @pl.loop(0, TOK // bt, init_carry=jnp.zeros((FP, HS), f32))
    def pooled_sum(i, total):
        o = (mm(load_rows(probs, i), vh[...], NN) * row_factor(i, 1.0)).astype(bf16)
        store_rows(oh, i, o)
        give_pair(oh, i, lat_out, 3)
        return total + mm(load_cols(member, i), o, NN)

    pooled = pooled_sum * inv_count
    square = jnp.sum(pooled * pooled, axis=1, keepdims=True)
    pooled_b = pooled.astype(bf16)
    for n in range(DH // 512):
        cols = pl.ds(n * 512, 512)
        rs_src[:, cols] = mm(pooled_b, w_ref[:, cols], NN).astype(bf16)
    lane_o = lax.broadcasted_iota(jnp.int32, (FP, OT), 1)

    def high_low(value):
        high = value.astype(bf16).astype(f32)
        return jnp.where(lane_o == 0, high, jnp.where(lane_o == 1, value - high, 0.0))

    rs_src[:, DH:] = high_low(square).astype(bf16)
    owner = chip + 16 * c

    for off in FAR:
        p = peer(off)
        o = p // 2 + 16 * (p % 2)

        @pl.when(o < OWN)
        def _():
            remote(
                rs_src.at[:, rows(o, OT)], rs_recv.at[rows(g, FP), :],
                sem_send.at[4], sem_recv.at[4], p,
            ).start()

    @pl.when(owner < OWN)
    def _():
        pltpu.make_async_copy(
            rs_src.at[:, rows(owner, OT)], rs_recv.at[rows(g, FP), :], sem_recv.at[4]
        ).start()

    def frame_sums(lo, hi):
        for n in range(lo, hi):
            cols = pl.ds(n * 512, 512)
            rbuf[:, cols] = mm(memberl[...], probs[:, cols], NN).astype(bf16)

    frame_sums(0, 4)

    @pl.when(owner < OWN)
    def _():
        drain(rs_recv, sem_recv.at[4])
        total = jnp.zeros((FP, OT), f32)
        for n in range(GEN):
            total = total + rs_recv[n * FP:(n + 1) * FP, :].astype(f32)
        both = high_low(total[:, 0:1] + total[:, 1:2])
        total = jnp.where(owner == OWN - 1, both, total)
        ag_src[...] = total.astype(bf16)
        pltpu.make_async_copy(ag_src, proj.at[:, rows(owner, OT)], sem_recv.at[5]).start()
        for off in FAR:
            p = peer(off)
            remote(
                ag_src, proj.at[:, rows(owner, OT)], sem_send.at[5], sem_recv.at[5], p
            ).start()

    frame_sums(4, 8)
    pltpu.make_async_copy(rbuf.at[:, rows(g, TD)], r_all.at[rows(g, FP), :], sem_recv.at[6]).start()
    for off in FAR:
        p = peer(off)
        remote(
            rbuf.at[:, rows(p, TD)], r_all.at[rows(g, FP), :], sem_send.at[6], sem_recv.at[6], p
        ).start()
    drain(proj, sem_recv.at[5])

    squares = proj[:, DH:DH + 128].astype(f32)
    squares = squares[:, 0:1] + squares[:, 1:2]
    root = jnp.sqrt(squares / (GEN * HS) + EPS)
    inv_root = 1.0 / root
    score = jnp.zeros((FP, 1), f32)
    dot_sum = jnp.zeros((FP, 1), f32)
    raw = jnp.zeros((FP, HS), f32)
    for n in range(DH // 512):
        cols = pl.ds(n * 512, 512)
        hr = head_rows[:, cols]
        pre = proj[:, cols].astype(f32) * inv_root
        gate = jax.nn.sigmoid(pre)
        feature = pre * gate
        gsf[:, cols] = feature
        slope = hr * (gate + feature * (1.0 - gate))
        score = score + jnp.sum(feature * hr, axis=1, keepdims=True)
        dot_sum = dot_sum + jnp.sum(slope * pre, axis=1, keepdims=True)
        raw = raw + mm(slope.astype(bf16), w_ref[:, cols], NT)
    weight = (time_ref[0].astype(f32) + 1.0) / NSTEPS
    grad_score = -weight * jax.nn.sigmoid(-score) / FRAMES
    grad_pooled = (grad_score * inv_root) * raw
    grad_pooled = grad_pooled - (grad_score * dot_sum * inv_root * inv_root / (GEN * HS)) * pooled
    table = (TOK * (grad_pooled * inv_count)).astype(bf16)
    g_src[...] = table
    pltpu.make_async_copy(g_src, g_all.at[rows(g, FP), :], sem_recv.at[7]).start()
    for off in FAR:
        p = peer(off)
        remote(g_src, g_all.at[rows(g, FP), :], sem_send.at[7], sem_recv.at[7], p).start()

    first = 8
    cb = 1024
    dkt[...] = jnp.zeros_like(dkt)

    def grads_of(i):
        grad_rows = mm(load_cols(member, i), g_src[...], TN)
        delta = jnp.sum(grad_rows * load_rows(oh, i).astype(f32), axis=1, keepdims=True)
        qb = (load_cols(qwt, i).astype(f32) * (load_cols(wrow, i) * inv_scale)).astype(bf16)
        return grad_rows.astype(bf16), delta, qb

    @pl.loop(0, first)
    def _(i):
        grad_b, delta, qb = grads_of(i)
        acc = jnp.zeros((bt, HS), f32)
        for n in range(TOK // cb):
            cols = pl.ds(n * cb, cb)
            dp = mm(grad_b, vh[cols, :], NT)
            ds = (dp - delta).astype(bf16) * load_rows(probs, i, cols)
            acc = acc + mm(ds, kh[cols, :], NN)
            dkt[:, cols] += mm(qb, ds, NN)
        store_rows(qh, i, (acc * row_factor(i, inv_scale)).astype(bf16))
        give_pair(qh, i, dq_out, 9)

    @pl.loop(0, 16)
    def _(i):
        ch = q_chip(i, -1)
        r = rows(ch, bq)
        kh[r, :] = jnp.transpose(dkt[:, r]).astype(bf16)
        give(kh, ch, dk_out, 10)

    for n in range(DH // 512):
        cols = pl.ds(n * 512, 512)
        value = grad_score * gsf[:, cols]
        high = value.astype(bf16)
        low = (value - high.astype(f32)).astype(bf16)
        hp_src[:, cols] = (mm(picked_t, high, NN) + mm(picked_t, low, NN)).astype(bf16)
    pltpu.make_async_copy(hp_src, hp_all.at[rows(x, 16), :], sem_recv.at[8]).start()
    for d in range(1, GRP):
        pltpu.make_async_remote_copy(
            src_ref=hp_src, dst_ref=hp_all.at[rows(x, 16), :],
            send_sem=sem_send.at[8], recv_sem=sem_recv.at[8],
            device_id={"grp": (x + d) % GRP}, device_id_type=MESH,
        ).start()

    drain(r_all, sem_recv.at[6])
    drain(g_all, sem_recv.at[7])
    for h in range(GEN):
        hr = pl.ds(h * FP, FP)
        qwt[:, h * HS:(h + 1) * HS] = mm(r_all[hr, :], g_all[hr, :], TN).astype(bf16)
    to_dv = pltpu.make_async_copy(qwt, dv_out, sem_recv.at[1])
    to_dv.start()
    drain(hp_all, sem_recv.at[8])
    total = jnp.zeros((16, DH), f32)
    for n in range(GRP):
        total = total + hp_all[n * 16:(n + 1) * 16, :].astype(f32)
    gh_out[...] = total[:NDH, :]

    to_dv.wait()
    drain(lat_out, sem_recv.at[3])
    drain(dq_out, sem_recv.at[9])
    drain(dk_out, sem_recv.at[10])
    sent = kh.at[pl.ds(0, (GEN - 1) * TD), :]
    for n in (0, 1, 2, 3, 9, 10):
        drain(sent, sem_send.at[n])

    @pl.when(owner < OWN)
    def _():
        drain(rs_src.at[:, pl.ds(0, (OWN - 1) * OT)], sem_send.at[4])
        drain(rs_recv.at[pl.ds(0, (GEN - 1) * FP), :], sem_send.at[5])

    @pl.when(owner >= OWN)
    def _():
        drain(rs_src, sem_send.at[4])

    drain(r_all.at[pl.ds(0, (GEN - 1) * FP), :], sem_send.at[6])
    drain(g_all.at[pl.ds(0, (GEN - 1) * FP), :], sem_send.at[7])
    drain(hp_all.at[pl.ds(0, (GRP - 1) * 16), :], sem_send.at[8])


def settle(*refs):
    n = 5
    ins, outs, bufs = refs[:n], refs[n:2 * n], refs[2 * n:3 * n]
    sem_in, sem_out = refs[3 * n:]
    pieces = []
    for i in range(n):
        parts = 4 if i < n - 1 else 1
        step = ins[i].shape[0] // parts
        pieces += [(i, pl.ds(j * step, step)) for j in range(parts)]
    moves = [
        (
            pltpu.make_async_copy(ins[i].at[r], bufs[i].at[r], sem_in.at[m]),
            pltpu.make_async_copy(bufs[i].at[r], outs[i].at[r], sem_out.at[m]),
        )
        for m, (i, r) in enumerate(pieces)
    ]
    for fetch, _ in moves:
        fetch.start()
    for fetch, put in moves:
        fetch.wait()
        put.start()
    for _, put in moves:
        put.wait()


def on_device(
    query_in, key_in, value_in, teacher_w, disc_heads, frame_of_token, head_of_frame, timestep
):
    vmem = pl.BlockSpec(memory_space=pltpu.VMEM)
    smem = pl.BlockSpec(memory_space=pltpu.SMEM)
    hbm = pl.BlockSpec(memory_space=pl.ANY)
    rows_shape = jax.ShapeDtypeStruct((TD, GEN * HS), bf16)
    V = pltpu.VMEM
    outs = pl.pallas_call(
        body,
        out_shape=(
            rows_shape, rows_shape, rows_shape, rows_shape,
            jax.ShapeDtypeStruct((NDH, DH), f32),
        ),
        in_specs=[hbm, hbm, hbm, vmem, vmem, vmem, smem, smem],
        out_specs=(hbm, hbm, hbm, hbm, vmem),
        scratch_shapes=[
            V((TOK, TOK), bf16),
            V((TOK, HS), bf16), V((TOK, HS), bf16), V((TOK, HS), bf16), V((TOK, HS), bf16),
            V((256, TOK), f32), V((256, TOK), f32),
            V((HS, TOK), f32), V((HS, TOK), bf16), V((1, TOK), f32),
            V((FP, TOK), bf16), V((FP, TOK), bf16), V((FP, TOK), bf16),
            V((GEN * FP, TD), bf16), V((FP, HS), bf16), V((GEN * FP, HS), bf16),
            V((FP, DH + OT), bf16), V((GEN * FP, OT), bf16), V((FP, OT), bf16),
            V((FP, DH + OT), bf16), V((FP, DH), f32), V((FP, DH), f32),
            V((16, DH), bf16), V((GRP * 16, DH), bf16),
            pltpu.SemaphoreType.DMA((11,)),
            pltpu.SemaphoreType.DMA((16,)),
            pltpu.SemaphoreType.DMA((11,)),
        ],
        compiler_params=pltpu.CompilerParams(
            collective_id=0, has_side_effects=True, vmem_limit_bytes=63 * 1024 * 1024
        ),
        name="clip_step",
    )(
        query_in[0], key_in[0], value_in[0], teacher_w, disc_heads,
        frame_of_token, head_of_frame, timestep,
    )
    lat, dq, dk, dv, gh = pl.pallas_call(
        settle,
        out_shape=tuple(jax.ShapeDtypeStruct(o.shape, o.dtype) for o in outs),
        in_specs=[hbm] * 5,
        out_specs=(hbm,) * 5,
        scratch_shapes=[V(o.shape, o.dtype) for o in outs] + [pltpu.SemaphoreType.DMA((17,))] * 2,
        name="settle",
    )(*outs)
    return (lat[None], dq[None], dk[None], dv[None], gh)


def solution(mesh):
    return jax.shard_map(
        on_device,
        mesh=mesh,
        in_specs=(
            P("grp", "gen", None),
            P("grp", "gen", None),
            P("grp", "gen", None),
            P("gen", None),
            P(),
            P("grp", None),
            P("grp", None),
            P("grp"),
        ),
        out_specs=(
            P("grp", "gen", None),
            P("grp", "gen", None),
            P("grp", "gen", None),
            P("grp", "gen", None),
            P(),
        ),
        check_vma=False,
    )
```

```python
import functools
import math

import jax
import jax.numpy as jnp
from jax import lax
from jax.experimental import pallas as pl
from jax.experimental.pallas import tpu as pltpu
from jax.sharding import PartitionSpec as P

HS = 128
FRAMES = 21
NDH = 8
NSTEPS = 1000
EPS = 1e-06
GEN = 32
GRP = 4
TOK = 4096
TD = 128
DH = 5120
FP = 32
OT = 256
OWN = 21
MESH = pl.DeviceIdType.MESH
f32 = jnp.float32
bf16 = jnp.bfloat16
NT = (((1,), (1,)), ((), ()))
NN = (((1,), (0,)), ((), ()))
TN = (((0,), (0,)), ((), ()))
CHIPS = [
    (2, 2), (3, 2), (2, 3), (1, 2), (2, 1), (0, 2), (2, 0), (3, 1), (1, 3), (3, 3), (1, 1),
    (0, 3), (0, 1), (3, 0), (1, 0),
]
FAR = [(dy, dz, dc) for dy, dz in CHIPS for dc in (0, 1)] + [(0, 0, 1)]


def mm(a, b, dims):
    return lax.dot_general(a, b, dims, preferred_element_type=f32)


def body(
    q_in, k_in, v_in, w_ref, disc_ref, frames_ref, hof_ref, time_ref,
    lat_out, dq_out, dk_out, dv_out, gh_out,
    probs, qh, kh, vh, oh, sa, sb, dkt, qwt, wrow, member, memberl, rbuf, r_all, g_src, g_all,
    rs_src, rs_recv, ag_src, proj, head_rows, gsf, hp_src, hp_all, dob,
    sem_send, sem_q, sem_recv,
):
    g = lax.axis_index("gen")
    x = lax.axis_index("grp")
    y = g // 8
    z = (g // 2) % 4
    c = g % 2
    chip = g // 2

    def peer(off):
        dy, dz, dc = off
        ey = dy + c * (dz - dy)
        ez = dz + c * (dy - dz)
        return ((y + ey) % 4) * 8 + ((z + ez) % 4) * 2 + (c + dc) % 2

    def rows(i, n):
        return pl.ds(pl.multiple_of(i * n, n), n)

    def remote(src, dst, send, recv, dev):
        return pltpu.make_async_remote_copy(
            src_ref=src, dst_ref=dst, send_sem=send, recv_sem=recv,
            device_id={"gen": dev}, device_id_type=MESH,
        )

    def drain(ref, sem):
        pltpu.make_async_copy(ref, ref, sem).wait()

    barrier = pltpu.get_barrier_semaphore()
    for off in FAR:
        pl.semaphore_signal(barrier, inc=1, device_id={"gen": peer(off)}, device_id_type=MESH)
    for d in range(1, GRP):
        pl.semaphore_signal(
            barrier, inc=1, device_id={"grp": (x + d) % GRP}, device_id_type=MESH
        )
    pl.semaphore_wait(barrier, GEN - 1 + GRP - 1)

    def q_chip(i, sign):
        dy = i % 4
        dz = (i // 4 + i) % 4
        return ((y + sign * dy + 4) % 4) * 4 + (z + sign * dz + 4) % 4

    def gather_rows(src, dst, which):
        pltpu.make_async_copy(
            src.at[:, rows(g, TD)], dst.at[rows(g, TD), :], sem_recv.at[which]
        ).start()
        for off in FAR:
            p = peer(off)
            remote(
                src.at[:, rows(p, TD)], dst.at[rows(g, TD), :],
                sem_send.at[which], sem_recv.at[which], p,
            ).start()

    gather_rows(k_in, kh, 0)
    pltpu.make_async_copy(q_in.at[:, rows(g, TD)], qh.at[rows(g, TD), :], sem_q.at[0]).start()
    for i in range(16):
        for dc in (0, 1):
            if i == 0 and dc == 0:
                continue
            p = q_chip(i, 1) * 2 + (c + dc) % 2
            remote(
                q_in.at[:, rows(p, TD)], qh.at[rows(g, TD), :], sem_send.at[2], sem_q.at[i], p
            ).start()
    gather_rows(v_in, vh, 1)

    frames = frames_ref[...]
    mem = (frames == lax.broadcasted_iota(jnp.int32, (FP, TOK), 0)).astype(f32)
    member[...] = mem.astype(bf16)
    counts = jnp.sum(mem, axis=1, keepdims=True)
    inv_count = jnp.where(counts > 0.0, 1.0 / jnp.maximum(counts, 1.0), 0.0)
    lane_n = lax.broadcasted_iota(jnp.int32, (FP, 128), 1)
    sub_n = lax.broadcasted_iota(jnp.int32, (FP, 128), 0)
    lane_8 = lax.broadcasted_iota(jnp.int32, (16, 128), 1)
    sub_8 = lax.broadcasted_iota(jnp.int32, (16, 128), 0)
    picked = jnp.zeros((FP, 128), f32)
    picked_t = jnp.zeros((16, 128), f32)
    for f in range(FRAMES):
        j = hof_ref[0, f]
        picked = jnp.where((sub_n == f) & (lane_n == j), 1.0, picked)
        picked_t = jnp.where((lane_8 == f) & (sub_8 == j), 1.0, picked_t)
    picked = picked[:, :NDH].astype(bf16)
    picked_t = picked_t[:, :FP].astype(bf16)
    for n in range(DH // 512):
        cols = pl.ds(n * 512, 512)
        part = disc_ref[:, cols]
        total = jnp.zeros((FP, 512), f32)
        for _ in range(3):
            high = part.astype(bf16)
            total = total + mm(picked, high, NN)
            part = part - high.astype(f32)
        head_rows[:, cols] = total

    scale2 = math.log2(math.e) / math.sqrt(HS)
    ck = 512
    bq = 256

    def step(i_s, s_write, i_p, s_read, peak):
        if i_s is not None:
            drain(qh.at[pl.ds(0, bq), :], sem_q.at[i_s])
            rs = rows(q_chip(i_s, -1), bq)
            qb = qh[rs, :]
            top = jnp.full((bq, 128), -jnp.inf, f32)
            qwt[:, rs] = jnp.transpose(qb.astype(f32)).astype(bf16)
        if i_p is not None:
            r = rows(q_chip(i_p, -1), bq)
            l = jnp.zeros((bq, 128), f32)
        for n in range(TOK // ck):
            cols = pl.ds(n * ck, ck)
            if i_s is not None:
                sn = mm(qb, kh[cols, :], NT)
                s_write[:, cols] = sn
                for j in range(ck // 128):
                    top = jnp.maximum(top, sn[:, j * 128:(j + 1) * 128])
            if i_p is not None:
                p = jnp.exp2((s_read[:, cols] - peak) * scale2)
                for j in range(ck // 128):
                    l = l + p[:, j * 128:(j + 1) * 128]
                probs[r, cols] = p.astype(bf16)
        if i_p is not None:
            wrow[:, r] = 1.0 / jnp.sum(jnp.transpose(l), axis=0, keepdims=True)
        if i_s is not None:
            return jnp.max(top, axis=1, keepdims=True)

    drain(kh, sem_recv.at[0])
    peak0 = step(0, sa, None, None, None)

    @pl.loop(0, 7, init_carry=peak0)
    def fwd(i, peak):
        peak1 = step(2 * i + 1, sb, 2 * i, sa, peak)
        return step(2 * i + 2, sa, 2 * i + 1, sb, peak1)

    peak15 = step(15, sb, 14, sa, fwd)
    step(None, None, 15, sb, peak15)

    bt = 512
    inv_scale = 1.0 / math.sqrt(HS)
    mine = pl.ds(pl.multiple_of(g * HS, HS), HS)

    def pair(i):
        return rows(q_chip(2 * i, -1), bq), rows(q_chip(2 * i + 1, -1), bq)

    def load_rows(ref, i, cols=slice(None)):
        r0, r1 = pair(i)
        return jnp.concatenate([ref[r0, cols], ref[r1, cols]], axis=0)

    def load_cols(ref, i):
        r0, r1 = pair(i)
        return jnp.concatenate([ref[:, r0], ref[:, r1]], axis=1)

    def store_rows(ref, i, value):
        r0, r1 = pair(i)
        ref[r0, :] = value[:bq]
        ref[r1, :] = value[bq:]

    def row_factor(i, factor):
        return jnp.transpose(jnp.broadcast_to(load_cols(wrow, i) * factor, (HS, bt)))

    def give(src, ch, out, which):
        other = ch * 2 + (1 - c)
        same = ch * 2 + c
        remote(
            src.at[rows(other, TD), :], out.at[:, mine], sem_send.at[which], sem_recv.at[which], other
        ).start()

        @pl.when(ch != chip)
        def _():
            remote(
                src.at[rows(same, TD), :], out.at[:, mine], sem_send.at[which], sem_recv.at[which], same
            ).start()

        @pl.when(ch == chip)
        def _():
            pltpu.make_async_copy(
                src.at[rows(same, TD), :], out.at[:, mine], sem_recv.at[which]
            ).start()

    def give_pair(src, i, out, which):
        give(src, q_chip(2 * i, -1), out, which)
        give(src, q_chip(2 * i + 1, -1), out, which)

    memberl[...] = (member[...].astype(f32) * wrow[...]).astype(bf16)
    drain(vh, sem_recv.at[1])

    @pl.loop(0, TOK // bt, init_carry=jnp.zeros((FP, HS), f32))
    def pooled_sum(i, total):
        o = (mm(load_rows(probs, i), vh[...], NN) * row_factor(i, 1.0)).astype(bf16)
        store_rows(oh, i, o)

        @pl.when(i < 5)
        def _():
            give_pair(oh, i, lat_out, 3)

        return total + mm(load_cols(member, i), o, NN)

    pooled = pooled_sum * inv_count
    square = jnp.sum(pooled * pooled, axis=1, keepdims=True)
    pooled_b = pooled.astype(bf16)
    for n in range(DH // 512):
        cols = pl.ds(n * 512, 512)
        rs_src[:, cols] = mm(pooled_b, w_ref[:, cols], NN).astype(bf16)
    lane_o = lax.broadcasted_iota(jnp.int32, (FP, OT), 1)

    def high_low(value):
        high = value.astype(bf16).astype(f32)
        return jnp.where(lane_o == 0, high, jnp.where(lane_o == 1, value - high, 0.0))

    rs_src[:, DH:] = high_low(square).astype(bf16)

    def owner_of(p):
        ch = p // 2
        second = jnp.where(ch % 5 == 0, 16 + ch // 5, jnp.where(ch == 4, OWN - 1, 2 * OWN))
        return jnp.where(p % 2 == 0, ch, second)

    owner = owner_of(g)

    for off in FAR:
        p = peer(off)
        o = owner_of(p)

        @pl.when(o < OWN)
        def _():
            remote(
                rs_src.at[:, rows(o, OT)], rs_recv.at[rows(g, FP), :],
                sem_send.at[4], sem_recv.at[4], p,
            ).start()

    @pl.when(owner < OWN)
    def _():
        pltpu.make_async_copy(
            rs_src.at[:, rows(owner, OT)], rs_recv.at[rows(g, FP), :], sem_recv.at[4]
        ).start()

    def frame_sums(lo, hi):
        for n in range(lo, hi):
            cols = pl.ds(n * 512, 512)
            rbuf[:, cols] = mm(memberl[...], probs[:, cols], NN).astype(bf16)

    frame_sums(0, 4)

    @pl.when(owner < OWN)
    def _():
        drain(rs_recv, sem_recv.at[4])
        total = jnp.zeros((FP, OT), f32)
        for n in range(GEN):
            total = total + rs_recv[n * FP:(n + 1) * FP, :].astype(f32)
        both = high_low(total[:, 0:1] + total[:, 1:2])
        total = jnp.where(owner == OWN - 1, both, total)
        ag_src[...] = total.astype(bf16)
        pltpu.make_async_copy(ag_src, proj.at[:, rows(owner, OT)], sem_recv.at[5]).start()
        for off in FAR:
            p = peer(off)
            remote(
                ag_src, proj.at[:, rows(owner, OT)], sem_send.at[5], sem_recv.at[5], p
            ).start()

    frame_sums(4, 8)
    drain(proj, sem_recv.at[5])

    squares = proj[:, DH:DH + 128].astype(f32)
    squares = squares[:, 0:1] + squares[:, 1:2]
    root = jnp.sqrt(squares / (GEN * HS) + EPS)
    inv_root = 1.0 / root
    score = jnp.zeros((FP, 1), f32)
    dot_sum = jnp.zeros((FP, 1), f32)
    raw = jnp.zeros((FP, HS), f32)
    for n in range(DH // 512):
        cols = pl.ds(n * 512, 512)
        hr = head_rows[:, cols]
        pre = proj[:, cols].astype(f32) * inv_root
        gate = jax.nn.sigmoid(pre)
        feature = pre * gate
        gsf[:, cols] = feature
        slope = hr * (gate + feature * (1.0 - gate))
        score = score + jnp.sum(feature * hr, axis=1, keepdims=True)
        dot_sum = dot_sum + jnp.sum(slope * pre, axis=1, keepdims=True)
        raw = raw + mm(slope.astype(bf16), w_ref[:, cols], NT)
    weight = (time_ref[0].astype(f32) + 1.0) / NSTEPS
    grad_score = -weight * jax.nn.sigmoid(-score) / FRAMES
    grad_pooled = (grad_score * inv_root) * raw
    grad_pooled = grad_pooled - (grad_score * dot_sum * inv_root * inv_root / (GEN * HS)) * pooled
    table = (TOK * (grad_pooled * inv_count)).astype(bf16)
    g_src[...] = table
    pltpu.make_async_copy(g_src, g_all.at[rows(g, FP), :], sem_recv.at[7]).start()
    for off in FAR:
        p = peer(off)
        remote(g_src, g_all.at[rows(g, FP), :], sem_send.at[7], sem_recv.at[7], p).start()

    for i in range(5, 8):
        give_pair(oh, i, lat_out, 3)
    pltpu.make_async_copy(rbuf.at[:, rows(g, TD)], r_all.at[rows(g, FP), :], sem_recv.at[6]).start()
    for off in FAR:
        p = peer(off)
        remote(
            rbuf.at[:, rows(p, TD)], r_all.at[rows(g, FP), :], sem_send.at[6], sem_recv.at[6], p
        ).start()

    first = 4
    cb = 1024
    dkt[...] = jnp.zeros_like(dkt)

    def grads_of(i):
        grad_rows = mm(load_cols(member, i), g_src[...], TN)
        delta = jnp.sum(grad_rows * load_rows(oh, i).astype(f32), axis=1, keepdims=True)
        qb = (load_cols(qwt, i).astype(f32) * (load_cols(wrow, i) * inv_scale)).astype(bf16)
        return grad_rows.astype(bf16), delta, qb

    @pl.loop(0, first)
    def _(i):
        grad_b, delta, qb = grads_of(i)
        acc = jnp.zeros((bt, HS), f32)
        for n in range(TOK // cb):
            cols = pl.ds(n * cb, cb)
            dp = mm(grad_b, vh[cols, :], NT)
            ds = (dp - delta).astype(bf16) * load_rows(probs, i, cols)
            acc = acc + mm(ds, kh[cols, :], NN)
            dkt[:, cols] += mm(qb, ds, NN)
        store_rows(qh, i, (acc * row_factor(i, inv_scale)).astype(bf16))
        give_pair(qh, i, dq_out, 9)

    def part(j, k):
        return pl.ds((2 * j + k) * HS, HS)

    def store_part(ref, j, value):
        ref[:, part(j, 0)] = value[:bq, :]
        ref[:, part(j, 1)] = value[bq:, :]

    def load_part(ref, j):
        return jnp.concatenate([ref[:, part(j, 0)], ref[:, part(j, 1)]], axis=0)

    rest = TOK // bt - first
    for j in range(rest):
        grad_b, delta, qb = grads_of(first + j)
        dob[j * bt:(j + 1) * bt, :] = grad_b
        store_part(sb, j, jnp.broadcast_to(delta, (bt, HS)))
        store_part(sa, j, jnp.zeros((bt, HS), f32))
        r0, r1 = pair(first + j)
        qwt[:, r0] = qb[:, :bq]
        qwt[:, r1] = qb[:, bq:]

    @pl.loop(0, 4)
    def _(i):
        chips = [q_chip(4 * i + m, -1) for m in range(4)]
        spans = [rows(ch, bq) for ch in chips]
        kc = jnp.concatenate([kh[r, :] for r in spans], axis=0)
        vc = jnp.concatenate([vh[r, :] for r in spans], axis=0)
        for j in range(rest):
            dp = mm(dob[j * bt:(j + 1) * bt, :], vc, NT)
            pb = jnp.concatenate([load_rows(probs, first + j, r) for r in spans], axis=1)
            ds = (dp - load_part(sb, j)[:, 0:1]).astype(bf16) * pb
            store_part(sa, j, load_part(sa, j) + mm(ds, kc, NN))
            dk = mm(load_cols(qwt, first + j), ds, NN)
            for m in range(4):
                dkt[:, spans[m]] += dk[:, m * bq:(m + 1) * bq]
        for m in range(4):
            kh[spans[m], :] = jnp.transpose(dkt[:, spans[m]]).astype(bf16)
            give(kh, chips[m], dk_out, 10)

    for j in range(rest):
        i = first + j
        store_rows(qh, i, (load_part(sa, j) * row_factor(i, inv_scale)).astype(bf16))
        give_pair(qh, i, dq_out, 9)

    for n in range(DH // 512):
        cols = pl.ds(n * 512, 512)
        value = grad_score * gsf[:, cols]
        high = value.astype(bf16)
        low = (value - high.astype(f32)).astype(bf16)
        hp_src[:, cols] = (mm(picked_t, high, NN) + mm(picked_t, low, NN)).astype(bf16)
    pltpu.make_async_copy(hp_src, hp_all.at[rows(x, 16), :], sem_recv.at[8]).start()
    for d in range(1, GRP):
        pltpu.make_async_remote_copy(
            src_ref=hp_src, dst_ref=hp_all.at[rows(x, 16), :],
            send_sem=sem_send.at[8], recv_sem=sem_recv.at[8],
            device_id={"grp": (x + d) % GRP}, device_id_type=MESH,
        ).start()

    drain(r_all, sem_recv.at[6])
    drain(g_all, sem_recv.at[7])
    for h in range(GEN):
        hr = pl.ds(h * FP, FP)
        qwt[:, h * HS:(h + 1) * HS] = mm(r_all[hr, :], g_all[hr, :], TN).astype(bf16)
    to_dv = pltpu.make_async_copy(qwt, dv_out, sem_recv.at[1])
    to_dv.start()
    drain(hp_all, sem_recv.at[8])
    total = jnp.zeros((16, DH), f32)
    for n in range(GRP):
        total = total + hp_all[n * 16:(n + 1) * 16, :].astype(f32)
    gh_out[...] = total[:NDH, :]

    to_dv.wait()
    drain(lat_out, sem_recv.at[3])
    drain(dq_out, sem_recv.at[9])
    drain(dk_out, sem_recv.at[10])
    sent = kh.at[pl.ds(0, (GEN - 1) * TD), :]
    for n in (0, 1, 2, 3, 9, 10):
        drain(sent, sem_send.at[n])

    @pl.when(owner < OWN)
    def _():
        drain(rs_src.at[:, pl.ds(0, (OWN - 1) * OT)], sem_send.at[4])
        drain(rs_recv.at[pl.ds(0, (GEN - 1) * FP), :], sem_send.at[5])

    @pl.when(owner >= OWN)
    def _():
        drain(rs_src, sem_send.at[4])

    drain(r_all.at[pl.ds(0, (GEN - 1) * FP), :], sem_send.at[6])
    drain(g_all.at[pl.ds(0, (GEN - 1) * FP), :], sem_send.at[7])
    drain(hp_all.at[pl.ds(0, (GRP - 1) * 16), :], sem_send.at[8])


def settle(*refs):
    n = 5
    ins, outs, bufs = refs[:n], refs[n:2 * n], refs[2 * n:3 * n]
    sem_in, sem_out = refs[3 * n:]
    pieces = []
    for i in range(n):
        parts = 4 if i < n - 1 else 1
        step = ins[i].shape[0] // parts
        pieces += [(i, pl.ds(j * step, step)) for j in range(parts)]
    moves = [
        (
            pltpu.make_async_copy(ins[i].at[r], bufs[i].at[r], sem_in.at[m]),
            pltpu.make_async_copy(bufs[i].at[r], outs[i].at[r], sem_out.at[m]),
        )
        for m, (i, r) in enumerate(pieces)
    ]
    for fetch, _ in moves:
        fetch.start()
    for fetch, put in moves:
        fetch.wait()
        put.start()
    for _, put in moves:
        put.wait()


def on_device(
    query_in, key_in, value_in, teacher_w, disc_heads, frame_of_token, head_of_frame, timestep
):
    vmem = pl.BlockSpec(memory_space=pltpu.VMEM)
    smem = pl.BlockSpec(memory_space=pltpu.SMEM)
    hbm = pl.BlockSpec(memory_space=pl.ANY)
    rows_shape = jax.ShapeDtypeStruct((TD, GEN * HS), bf16)
    V = pltpu.VMEM
    outs = pl.pallas_call(
        body,
        out_shape=(
            rows_shape, rows_shape, rows_shape, rows_shape,
            jax.ShapeDtypeStruct((NDH, DH), f32),
        ),
        in_specs=[hbm, hbm, hbm, vmem, vmem, vmem, smem, smem],
        out_specs=(hbm, hbm, hbm, hbm, vmem),
        scratch_shapes=[
            V((TOK, TOK), bf16),
            V((TOK, HS), bf16), V((TOK, HS), bf16), V((TOK, HS), bf16), V((TOK, HS), bf16),
            V((256, TOK), f32), V((256, TOK), f32),
            V((HS, TOK), f32), V((HS, TOK), bf16), V((1, TOK), f32),
            V((FP, TOK), bf16), V((FP, TOK), bf16), V((FP, TOK), bf16),
            V((GEN * FP, TD), bf16), V((FP, HS), bf16), V((GEN * FP, HS), bf16),
            V((FP, DH + OT), bf16), V((GEN * FP, OT), bf16), V((FP, OT), bf16),
            V((FP, DH + OT), bf16), V((FP, DH), f32), V((FP, DH), f32),
            V((16, DH), bf16), V((GRP * 16, DH), bf16),
            V((TOK // 2, HS), bf16),
            pltpu.SemaphoreType.DMA((11,)),
            pltpu.SemaphoreType.DMA((16,)),
            pltpu.SemaphoreType.DMA((11,)),
        ],
        compiler_params=pltpu.CompilerParams(
            collective_id=0, has_side_effects=True, vmem_limit_bytes=63 * 1024 * 1024
        ),
        name="clip_step",
    )(
        query_in[0], key_in[0], value_in[0], teacher_w, disc_heads,
        frame_of_token, head_of_frame, timestep,
    )
    lat, dq, dk, dv, gh = pl.pallas_call(
        settle,
        out_shape=tuple(jax.ShapeDtypeStruct(o.shape, o.dtype) for o in outs),
        in_specs=[hbm] * 5,
        out_specs=(hbm,) * 5,
        scratch_shapes=[V(o.shape, o.dtype) for o in outs] + [pltpu.SemaphoreType.DMA((17,))] * 2,
        name="settle",
    )(*outs)
    return (lat[None], dq[None], dk[None], dv[None], gh)


def solution(mesh):
    return jax.shard_map(
        on_device,
        mesh=mesh,
        in_specs=(
            P("grp", "gen", None),
            P("grp", "gen", None),
            P("grp", "gen", None),
            P("gen", None),
            P(),
            P("grp", None),
            P("grp", None),
            P("grp"),
        ),
        out_specs=(
            P("grp", "gen", None),
            P("grp", "gen", None),
            P("grp", "gen", None),
            P("grp", "gen", None),
            P(),
        ),
        check_vma=False,
    )
```

```python
import functools
import math

import jax
import jax.numpy as jnp
from jax import lax
from jax.experimental import pallas as pl
from jax.experimental.pallas import tpu as pltpu
from jax.sharding import PartitionSpec as P

HS = 128
FRAMES = 21
NDH = 8
NSTEPS = 1000
EPS = 1e-06
GEN = 32
GRP = 4
TOK = 4096
TD = 128
DH = 5120
FP = 32
OT = 256
OWN = 21
MESH = pl.DeviceIdType.MESH
f32 = jnp.float32
bf16 = jnp.bfloat16
NT = (((1,), (1,)), ((), ()))
NN = (((1,), (0,)), ((), ()))
TN = (((0,), (0,)), ((), ()))
CHIPS = [
    (2, 2), (3, 2), (2, 3), (1, 2), (2, 1), (0, 2), (2, 0), (3, 1), (1, 3), (3, 3), (1, 1),
    (0, 3), (0, 1), (3, 0), (1, 0),
]
FAR = [(dy, dz, dc) for dy, dz in CHIPS for dc in (0, 1)] + [(0, 0, 1)]


def mm(a, b, dims):
    return lax.dot_general(a, b, dims, preferred_element_type=f32)


def body(
    q_in, k_in, v_in, w_ref, disc_ref, frames_ref, hof_ref, time_ref,
    lat_out, dq_out, dk_out, dv_out, gh_out,
    probs, qh, kh, vh, oh, sa, sb, dkt, qwt, wrow, member, memberl, rbuf, r_all, g_src, g_all,
    rs_src, rs_recv, ag_src, proj, head_rows, gsf, hp_src, hp_all, dob,
    sem_send, sem_q, sem_recv,
):
    g = lax.axis_index("gen")
    x = lax.axis_index("grp")
    y = g // 8
    z = (g // 2) % 4
    c = g % 2
    chip = g // 2

    def peer(off):
        dy, dz, dc = off
        ey = dy + c * (dz - dy)
        ez = dz + c * (dy - dz)
        return ((y + ey) % 4) * 8 + ((z + ez) % 4) * 2 + (c + dc) % 2

    def rows(i, n):
        return pl.ds(pl.multiple_of(i * n, n), n)

    def remote(src, dst, send, recv, dev):
        return pltpu.make_async_remote_copy(
            src_ref=src, dst_ref=dst, send_sem=send, recv_sem=recv,
            device_id={"gen": dev}, device_id_type=MESH,
        )

    def drain(ref, sem):
        pltpu.make_async_copy(ref, ref, sem).wait()

    barrier = pltpu.get_barrier_semaphore()
    for off in FAR:
        pl.semaphore_signal(barrier, inc=1, device_id={"gen": peer(off)}, device_id_type=MESH)
    for d in range(1, GRP):
        pl.semaphore_signal(
            barrier, inc=1, device_id={"grp": (x + d) % GRP}, device_id_type=MESH
        )
    pl.semaphore_wait(barrier, GEN - 1 + GRP - 1)

    def q_chip(i, sign):
        dy = i % 4
        dz = (i // 4 + i) % 4
        return ((y + sign * dy + 4) % 4) * 4 + (z + sign * dz + 4) % 4

    def gather_rows(src, dst, which):
        pltpu.make_async_copy(
            src.at[:, rows(g, TD)], dst.at[rows(g, TD), :], sem_recv.at[which]
        ).start()
        for off in FAR:
            p = peer(off)
            remote(
                src.at[:, rows(p, TD)], dst.at[rows(g, TD), :],
                sem_send.at[which], sem_recv.at[which], p,
            ).start()

    gather_rows(k_in, kh, 0)

    frames = frames_ref[...]
    mem = (frames == lax.broadcasted_iota(jnp.int32, (FP, TOK), 0)).astype(f32)
    member[...] = mem.astype(bf16)
    counts = jnp.sum(mem, axis=1, keepdims=True)
    inv_count = jnp.where(counts > 0.0, 1.0 / jnp.maximum(counts, 1.0), 0.0)
    lane_n = lax.broadcasted_iota(jnp.int32, (FP, 128), 1)
    sub_n = lax.broadcasted_iota(jnp.int32, (FP, 128), 0)
    lane_8 = lax.broadcasted_iota(jnp.int32, (16, 128), 1)
    sub_8 = lax.broadcasted_iota(jnp.int32, (16, 128), 0)
    picked = jnp.zeros((FP, 128), f32)
    picked_t = jnp.zeros((16, 128), f32)
    for f in range(FRAMES):
        j = hof_ref[0, f]
        picked = jnp.where((sub_n == f) & (lane_n == j), 1.0, picked)
        picked_t = jnp.where((lane_8 == f) & (sub_8 == j), 1.0, picked_t)
    picked = picked[:, :NDH].astype(bf16)
    picked_t = picked_t[:, :FP].astype(bf16)
    for n in range(DH // 512):
        cols = pl.ds(n * 512, 512)
        part = disc_ref[:, cols]
        total = jnp.zeros((FP, 512), f32)
        for _ in range(3):
            high = part.astype(bf16)
            total = total + mm(picked, high, NN)
            part = part - high.astype(f32)
        head_rows[:, cols] = total

    pltpu.make_async_copy(q_in.at[:, rows(g, TD)], qh.at[rows(g, TD), :], sem_q.at[0]).start()
    for i in range(16):
        for dc in (0, 1):
            if i == 0 and dc == 0:
                continue
            p = q_chip(i, 1) * 2 + (c + dc) % 2
            remote(
                q_in.at[:, rows(p, TD)], qh.at[rows(g, TD), :], sem_send.at[2], sem_q.at[i], p
            ).start()

    scale2 = math.log2(math.e) / math.sqrt(HS)
    ck = 512
    bq = 256

    def step(i_s, s_write, i_p, s_read, peak):
        if i_s is not None:
            drain(qh.at[pl.ds(0, bq), :], sem_q.at[i_s])
            rs = rows(q_chip(i_s, -1), bq)
            qb = qh[rs, :]
            top = jnp.full((bq, 128), -jnp.inf, f32)
            qwt[:, rs] = jnp.transpose(qb.astype(f32)).astype(bf16)
        if i_p is not None:
            r = rows(q_chip(i_p, -1), bq)
            l = jnp.zeros((bq, 128), f32)
        for n in range(TOK // ck):
            cols = pl.ds(n * ck, ck)
            if i_s is not None:
                sn = mm(qb, kh[cols, :], NT)
                s_write[:, cols] = sn
                for j in range(ck // 128):
                    top = jnp.maximum(top, sn[:, j * 128:(j + 1) * 128])
            if i_p is not None:
                p = jnp.exp2((s_read[:, cols] - peak) * scale2)
                for j in range(ck // 128):
                    l = l + p[:, j * 128:(j + 1) * 128]
                probs[r, cols] = p.astype(bf16)
        if i_p is not None:
            wrow[:, r] = 1.0 / jnp.sum(jnp.transpose(l), axis=0, keepdims=True)
        if i_s is not None:
            return jnp.max(top, axis=1, keepdims=True)

    drain(kh, sem_recv.at[0])
    gather_rows(v_in, vh, 1)
    peak0 = step(0, sa, None, None, None)

    @pl.loop(0, 7, init_carry=peak0)
    def fwd(i, peak):
        peak1 = step(2 * i + 1, sb, 2 * i, sa, peak)
        return step(2 * i + 2, sa, 2 * i + 1, sb, peak1)

    peak15 = step(15, sb, 14, sa, fwd)
    step(None, None, 15, sb, peak15)

    bt = 512
    inv_scale = 1.0 / math.sqrt(HS)
    mine = pl.ds(pl.multiple_of(g * HS, HS), HS)

    def pair(i):
        return rows(q_chip(2 * i, -1), bq), rows(q_chip(2 * i + 1, -1), bq)

    def load_rows(ref, i, cols=slice(None)):
        r0, r1 = pair(i)
        return jnp.concatenate([ref[r0, cols], ref[r1, cols]], axis=0)

    def load_cols(ref, i):
        r0, r1 = pair(i)
        return jnp.concatenate([ref[:, r0], ref[:, r1]], axis=1)

    def store_rows(ref, i, value):
        r0, r1 = pair(i)
        ref[r0, :] = value[:bq]
        ref[r1, :] = value[bq:]

    def row_factor(i, factor):
        return jnp.transpose(jnp.broadcast_to(load_cols(wrow, i) * factor, (HS, bt)))

    def give(src, ch, out, which):
        other = ch * 2 + (1 - c)
        same = ch * 2 + c
        remote(
            src.at[rows(other, TD), :], out.at[:, mine], sem_send.at[which], sem_recv.at[which], other
        ).start()

        @pl.when(ch != chip)
        def _():
            remote(
                src.at[rows(same, TD), :], out.at[:, mine], sem_send.at[which], sem_recv.at[which], same
            ).start()

        @pl.when(ch == chip)
        def _():
            pltpu.make_async_copy(
                src.at[rows(same, TD), :], out.at[:, mine], sem_recv.at[which]
            ).start()

    def give_pair(src, i, out, which):
        give(src, q_chip(2 * i, -1), out, which)
        give(src, q_chip(2 * i + 1, -1), out, which)

    memberl[...] = (member[...].astype(f32) * wrow[...]).astype(bf16)
    drain(vh, sem_recv.at[1])

    @pl.loop(0, TOK // bt, init_carry=jnp.zeros((FP, HS), f32))
    def pooled_sum(i, total):
        o = (mm(load_rows(probs, i), vh[...], NN) * row_factor(i, 1.0)).astype(bf16)
        store_rows(oh, i, o)

        @pl.when(i < 5)
        def _():
            give_pair(oh, i, lat_out, 3)

        return total + mm(load_cols(member, i), o, NN)

    pooled = pooled_sum * inv_count
    square = jnp.sum(pooled * pooled, axis=1, keepdims=True)
    pooled_b = pooled.astype(bf16)
    for n in range(DH // 512):
        cols = pl.ds(n * 512, 512)
        rs_src[:, cols] = mm(pooled_b, w_ref[:, cols], NN).astype(bf16)
    lane_o = lax.broadcasted_iota(jnp.int32, (FP, OT), 1)

    def high_low(value):
        high = value.astype(bf16).astype(f32)
        return jnp.where(lane_o == 0, high, jnp.where(lane_o == 1, value - high, 0.0))

    rs_src[:, DH:] = high_low(square).astype(bf16)

    def owner_of(p):
        ch = p // 2
        second = jnp.where(ch % 5 == 0, 16 + ch // 5, jnp.where(ch == 4, OWN - 1, 2 * OWN))
        return jnp.where(p % 2 == 0, ch, second)

    owner = owner_of(g)

    for off in FAR:
        p = peer(off)
        o = owner_of(p)

        @pl.when(o < OWN)
        def _():
            remote(
                rs_src.at[:, rows(o, OT)], rs_recv.at[rows(g, FP), :],
                sem_send.at[4], sem_recv.at[4], p,
            ).start()

    @pl.when(owner < OWN)
    def _():
        pltpu.make_async_copy(
            rs_src.at[:, rows(owner, OT)], rs_recv.at[rows(g, FP), :], sem_recv.at[4]
        ).start()

    def frame_sums(lo, hi):
        for n in range(lo, hi):
            cols = pl.ds(n * 512, 512)
            rbuf[:, cols] = mm(memberl[...], probs[:, cols], NN).astype(bf16)

    frame_sums(0, 4)

    @pl.when(owner < OWN)
    def _():
        drain(rs_recv, sem_recv.at[4])
        total = jnp.zeros((FP, OT), f32)
        for n in range(GEN):
            total = total + rs_recv[n * FP:(n + 1) * FP, :].astype(f32)
        both = high_low(total[:, 0:1] + total[:, 1:2])
        total = jnp.where(owner == OWN - 1, both, total)
        ag_src[...] = total.astype(bf16)
        pltpu.make_async_copy(ag_src, proj.at[:, rows(owner, OT)], sem_recv.at[5]).start()
        for off in FAR:
            p = peer(off)
            remote(
                ag_src, proj.at[:, rows(owner, OT)], sem_send.at[5], sem_recv.at[5], p
            ).start()

    frame_sums(4, 8)
    drain(proj, sem_recv.at[5])

    squares = proj[:, DH:DH + 128].astype(f32)
    squares = squares[:, 0:1] + squares[:, 1:2]
    root = jnp.sqrt(squares / (GEN * HS) + EPS)
    inv_root = 1.0 / root
    score = jnp.zeros((FP, 1), f32)
    dot_sum = jnp.zeros((FP, 1), f32)
    raw = jnp.zeros((FP, HS), f32)
    for n in range(DH // 512):
        cols = pl.ds(n * 512, 512)
        hr = head_rows[:, cols]
        pre = proj[:, cols].astype(f32) * inv_root
        gate = jax.nn.sigmoid(pre)
        feature = pre * gate
        gsf[:, cols] = feature
        slope = hr * (gate + feature * (1.0 - gate))
        score = score + jnp.sum(feature * hr, axis=1, keepdims=True)
        dot_sum = dot_sum + jnp.sum(slope * pre, axis=1, keepdims=True)
        raw = raw + mm(slope.astype(bf16), w_ref[:, cols], NT)
    weight = (time_ref[0].astype(f32) + 1.0) / NSTEPS
    grad_score = -weight * jax.nn.sigmoid(-score) / FRAMES
    grad_pooled = (grad_score * inv_root) * raw
    grad_pooled = grad_pooled - (grad_score * dot_sum * inv_root * inv_root / (GEN * HS)) * pooled
    table = (TOK * (grad_pooled * inv_count)).astype(bf16)
    g_src[...] = table
    pltpu.make_async_copy(g_src, g_all.at[rows(g, FP), :], sem_recv.at[7]).start()
    for off in FAR:
        p = peer(off)
        remote(g_src, g_all.at[rows(g, FP), :], sem_send.at[7], sem_recv.at[7], p).start()

    for i in range(5, 8):
        give_pair(oh, i, lat_out, 3)
    pltpu.make_async_copy(rbuf.at[:, rows(g, TD)], r_all.at[rows(g, FP), :], sem_recv.at[6]).start()
    for off in FAR:
        p = peer(off)
        remote(
            rbuf.at[:, rows(p, TD)], r_all.at[rows(g, FP), :], sem_send.at[6], sem_recv.at[6], p
        ).start()

    first = 4
    cb = 1024
    dkt[...] = jnp.zeros_like(dkt)

    def grads_of(i):
        grad_rows = mm(load_cols(member, i), g_src[...], TN)
        delta = jnp.sum(grad_rows * load_rows(oh, i).astype(f32), axis=1, keepdims=True)
        qb = (load_cols(qwt, i).astype(f32) * (load_cols(wrow, i) * inv_scale)).astype(bf16)
        return grad_rows.astype(bf16), delta, qb

    @pl.loop(0, first)
    def _(i):
        grad_b, delta, qb = grads_of(i)
        acc = jnp.zeros((bt, HS), f32)
        for n in range(TOK // cb):
            cols = pl.ds(n * cb, cb)
            dp = mm(grad_b, vh[cols, :], NT)
            ds = (dp - delta).astype(bf16) * load_rows(probs, i, cols)
            acc = acc + mm(ds, kh[cols, :], NN)
            dkt[:, cols] += mm(qb, ds, NN)
        store_rows(qh, i, (acc * row_factor(i, inv_scale)).astype(bf16))
        give_pair(qh, i, dq_out, 9)

    def part(j, k):
        return pl.ds((2 * j + k) * HS, HS)

    def store_part(ref, j, value):
        ref[:, part(j, 0)] = value[:bq, :]
        ref[:, part(j, 1)] = value[bq:, :]

    def load_part(ref, j):
        return jnp.concatenate([ref[:, part(j, 0)], ref[:, part(j, 1)]], axis=0)

    rest = TOK // bt - first
    for j in range(rest):
        grad_b, delta, qb = grads_of(first + j)
        dob[j * bt:(j + 1) * bt, :] = grad_b
        store_part(sb, j, jnp.broadcast_to(delta, (bt, HS)))
        store_part(sa, j, jnp.zeros((bt, HS), f32))
        r0, r1 = pair(first + j)
        qwt[:, r0] = qb[:, :bq]
        qwt[:, r1] = qb[:, bq:]

    @pl.loop(0, 4)
    def _(i):
        chips = [q_chip(4 * i + m, -1) for m in range(4)]
        spans = [rows(ch, bq) for ch in chips]
        kc = jnp.concatenate([kh[r, :] for r in spans], axis=0)
        vc = jnp.concatenate([vh[r, :] for r in spans], axis=0)
        for j in range(rest):
            dp = mm(dob[j * bt:(j + 1) * bt, :], vc, NT)
            pb = jnp.concatenate([load_rows(probs, first + j, r) for r in spans], axis=1)
            ds = (dp - load_part(sb, j)[:, 0:1]).astype(bf16) * pb
            store_part(sa, j, load_part(sa, j) + mm(ds, kc, NN))
            dk = mm(load_cols(qwt, first + j), ds, NN)
            for m in range(4):
                dkt[:, spans[m]] += dk[:, m * bq:(m + 1) * bq]
        for m in range(4):
            kh[spans[m], :] = jnp.transpose(dkt[:, spans[m]]).astype(bf16)
            give(kh, chips[m], dk_out, 10)

    for j in range(rest):
        i = first + j
        store_rows(qh, i, (load_part(sa, j) * row_factor(i, inv_scale)).astype(bf16))
        give_pair(qh, i, dq_out, 9)

    for n in range(DH // 512):
        cols = pl.ds(n * 512, 512)
        value = grad_score * gsf[:, cols]
        high = value.astype(bf16)
        low = (value - high.astype(f32)).astype(bf16)
        hp_src[:, cols] = (mm(picked_t, high, NN) + mm(picked_t, low, NN)).astype(bf16)
    pltpu.make_async_copy(hp_src, hp_all.at[rows(x, 16), :], sem_recv.at[8]).start()
    for d in range(1, GRP):
        pltpu.make_async_remote_copy(
            src_ref=hp_src, dst_ref=hp_all.at[rows(x, 16), :],
            send_sem=sem_send.at[8], recv_sem=sem_recv.at[8],
            device_id={"grp": (x + d) % GRP}, device_id_type=MESH,
        ).start()

    drain(r_all, sem_recv.at[6])
    drain(g_all, sem_recv.at[7])
    for h in range(GEN):
        hr = pl.ds(h * FP, FP)
        qwt[:, h * HS:(h + 1) * HS] = mm(r_all[hr, :], g_all[hr, :], TN).astype(bf16)
    to_dv = pltpu.make_async_copy(qwt, dv_out, sem_recv.at[1])
    to_dv.start()
    drain(hp_all, sem_recv.at[8])
    total = jnp.zeros((16, DH), f32)
    for n in range(GRP):
        total = total + hp_all[n * 16:(n + 1) * 16, :].astype(f32)
    gh_out[...] = total[:NDH, :]

    to_dv.wait()
    drain(lat_out, sem_recv.at[3])
    drain(dq_out, sem_recv.at[9])
    drain(dk_out, sem_recv.at[10])
    sent = kh.at[pl.ds(0, (GEN - 1) * TD), :]
    for n in (0, 1, 2, 3, 9, 10):
        drain(sent, sem_send.at[n])

    @pl.when(owner < OWN)
    def _():
        drain(rs_src.at[:, pl.ds(0, (OWN - 1) * OT)], sem_send.at[4])
        drain(rs_recv.at[pl.ds(0, (GEN - 1) * FP), :], sem_send.at[5])

    @pl.when(owner >= OWN)
    def _():
        drain(rs_src, sem_send.at[4])

    drain(r_all.at[pl.ds(0, (GEN - 1) * FP), :], sem_send.at[6])
    drain(g_all.at[pl.ds(0, (GEN - 1) * FP), :], sem_send.at[7])
    drain(hp_all.at[pl.ds(0, (GRP - 1) * 16), :], sem_send.at[8])


def settle(*refs):
    n = 5
    ins, outs, bufs = refs[:n], refs[n:2 * n], refs[2 * n:3 * n]
    sem_in, sem_out = refs[3 * n:]
    pieces = []
    for i in range(n):
        parts = 4 if i < n - 1 else 1
        step = ins[i].shape[0] // parts
        pieces += [(i, pl.ds(j * step, step)) for j in range(parts)]
    moves = [
        (
            pltpu.make_async_copy(ins[i].at[r], bufs[i].at[r], sem_in.at[m]),
            pltpu.make_async_copy(bufs[i].at[r], outs[i].at[r], sem_out.at[m]),
        )
        for m, (i, r) in enumerate(pieces)
    ]
    for fetch, _ in moves:
        fetch.start()
    for fetch, put in moves:
        fetch.wait()
        put.start()
    for _, put in moves:
        put.wait()


def on_device(
    query_in, key_in, value_in, teacher_w, disc_heads, frame_of_token, head_of_frame, timestep
):
    vmem = pl.BlockSpec(memory_space=pltpu.VMEM)
    smem = pl.BlockSpec(memory_space=pltpu.SMEM)
    hbm = pl.BlockSpec(memory_space=pl.ANY)
    rows_shape = jax.ShapeDtypeStruct((TD, GEN * HS), bf16)
    V = pltpu.VMEM
    outs = pl.pallas_call(
        body,
        out_shape=(
            rows_shape, rows_shape, rows_shape, rows_shape,
            jax.ShapeDtypeStruct((NDH, DH), f32),
        ),
        in_specs=[hbm, hbm, hbm, vmem, vmem, vmem, smem, smem],
        out_specs=(hbm, hbm, hbm, hbm, vmem),
        scratch_shapes=[
            V((TOK, TOK), bf16),
            V((TOK, HS), bf16), V((TOK, HS), bf16), V((TOK, HS), bf16), V((TOK, HS), bf16),
            V((256, TOK), f32), V((256, TOK), f32),
            V((HS, TOK), f32), V((HS, TOK), bf16), V((1, TOK), f32),
            V((FP, TOK), bf16), V((FP, TOK), bf16), V((FP, TOK), bf16),
            V((GEN * FP, TD), bf16), V((FP, HS), bf16), V((GEN * FP, HS), bf16),
            V((FP, DH + OT), bf16), V((GEN * FP, OT), bf16), V((FP, OT), bf16),
            V((FP, DH + OT), bf16), V((FP, DH), f32), V((FP, DH), f32),
            V((16, DH), bf16), V((GRP * 16, DH), bf16),
            V((TOK // 2, HS), bf16),
            pltpu.SemaphoreType.DMA((11,)),
            pltpu.SemaphoreType.DMA((16,)),
            pltpu.SemaphoreType.DMA((11,)),
        ],
        compiler_params=pltpu.CompilerParams(
            collective_id=0, has_side_effects=True, vmem_limit_bytes=63 * 1024 * 1024
        ),
        name="clip_step",
    )(
        query_in[0], key_in[0], value_in[0], teacher_w, disc_heads,
        frame_of_token, head_of_frame, timestep,
    )
    lat, dq, dk, dv, gh = pl.pallas_call(
        settle,
        out_shape=tuple(jax.ShapeDtypeStruct(o.shape, o.dtype) for o in outs),
        in_specs=[hbm] * 5,
        out_specs=(hbm,) * 5,
        scratch_shapes=[V(o.shape, o.dtype) for o in outs] + [pltpu.SemaphoreType.DMA((17,))] * 2,
        name="settle",
    )(*outs)
    return (lat[None], dq[None], dk[None], dv[None], gh)


def solution(mesh):
    return jax.shard_map(
        on_device,
        mesh=mesh,
        in_specs=(
            P("grp", "gen", None),
            P("grp", "gen", None),
            P("grp", "gen", None),
            P("gen", None),
            P(),
            P("grp", None),
            P("grp", None),
            P("grp"),
        ),
        out_specs=(
            P("grp", "gen", None),
            P("grp", "gen", None),
            P("grp", "gen", None),
            P("grp", "gen", None),
            P(),
        ),
        check_vma=False,
    )
```

```python
import functools
import math

import jax
import jax.numpy as jnp
from jax import lax
from jax.experimental import pallas as pl
from jax.experimental.pallas import tpu as pltpu
from jax.sharding import PartitionSpec as P

HS = 128
FRAMES = 21
NDH = 8
NSTEPS = 1000
EPS = 1e-06
GEN = 32
GRP = 4
TOK = 4096
TD = 128
DH = 5120
FP = 32
OT = 256
OWN = 21
MESH = pl.DeviceIdType.MESH
f32 = jnp.float32
bf16 = jnp.bfloat16
NT = (((1,), (1,)), ((), ()))
NN = (((1,), (0,)), ((), ()))
TN = (((0,), (0,)), ((), ()))
CHIPS = [
    (2, 2), (3, 2), (2, 3), (1, 2), (2, 1), (0, 2), (2, 0), (3, 1), (1, 3), (3, 3), (1, 1),
    (0, 3), (0, 1), (3, 0), (1, 0),
]
FAR = [(dy, dz, dc) for dy, dz in CHIPS for dc in (0, 1)] + [(0, 0, 1)]


def mm(a, b, dims):
    return lax.dot_general(a, b, dims, preferred_element_type=f32)


def body(
    q_in, k_in, v_in, w_ref, disc_ref, frames_ref, hof_ref, time_ref,
    lat_out, dq_out, dk_out, dv_out, gh_out,
    probs, qh, kh, vh, oh, sa, sb, dkt, qwt, wrow, member, memberl, rbuf, r_all, g_src, g_all,
    rs_src, rs_recv, ag_src, proj, head_rows, gsf, hp_src, hp_all, dob,
    sem_send, sem_q, sem_recv,
):
    g = lax.axis_index("gen")
    x = lax.axis_index("grp")
    y = g // 8
    z = (g // 2) % 4
    c = g % 2
    chip = g // 2

    def peer(off):
        dy, dz, dc = off
        ey = dy + c * (dz - dy)
        ez = dz + c * (dy - dz)
        return ((y + ey) % 4) * 8 + ((z + ez) % 4) * 2 + (c + dc) % 2

    def rows(i, n):
        return pl.ds(pl.multiple_of(i * n, n), n)

    def remote(src, dst, send, recv, dev):
        return pltpu.make_async_remote_copy(
            src_ref=src, dst_ref=dst, send_sem=send, recv_sem=recv,
            device_id={"gen": dev}, device_id_type=MESH,
        )

    def drain(ref, sem):
        pltpu.make_async_copy(ref, ref, sem).wait()

    barrier = pltpu.get_barrier_semaphore()
    for off in FAR:
        pl.semaphore_signal(barrier, inc=1, device_id={"gen": peer(off)}, device_id_type=MESH)
    for d in range(1, GRP):
        pl.semaphore_signal(
            barrier, inc=1, device_id={"grp": (x + d) % GRP}, device_id_type=MESH
        )
    pl.semaphore_wait(barrier, GEN - 1 + GRP - 1)

    def q_chip(i, sign):
        dy = i % 4
        dz = (i // 4 + i) % 4
        return ((y + sign * dy + 4) % 4) * 4 + (z + sign * dz + 4) % 4

    def gather_rows(src, dst, which):
        pltpu.make_async_copy(
            src.at[:, rows(g, TD)], dst.at[rows(g, TD), :], sem_recv.at[which]
        ).start()
        for off in FAR:
            p = peer(off)
            remote(
                src.at[:, rows(p, TD)], dst.at[rows(g, TD), :],
                sem_send.at[which], sem_recv.at[which], p,
            ).start()

    gather_rows(k_in, kh, 0)

    frames = frames_ref[...]
    mem = (frames == lax.broadcasted_iota(jnp.int32, (FP, TOK), 0)).astype(f32)
    member[...] = mem.astype(bf16)
    counts = jnp.sum(mem, axis=1, keepdims=True)
    inv_count = jnp.where(counts > 0.0, 1.0 / jnp.maximum(counts, 1.0), 0.0)
    lane_n = lax.broadcasted_iota(jnp.int32, (FP, 128), 1)
    sub_n = lax.broadcasted_iota(jnp.int32, (FP, 128), 0)
    lane_8 = lax.broadcasted_iota(jnp.int32, (16, 128), 1)
    sub_8 = lax.broadcasted_iota(jnp.int32, (16, 128), 0)
    picked = jnp.zeros((FP, 128), f32)
    picked_t = jnp.zeros((16, 128), f32)
    for f in range(FRAMES):
        j = hof_ref[0, f]
        picked = jnp.where((sub_n == f) & (lane_n == j), 1.0, picked)
        picked_t = jnp.where((lane_8 == f) & (sub_8 == j), 1.0, picked_t)
    picked = picked[:, :NDH].astype(bf16)
    picked_t = picked_t[:, :FP].astype(bf16)
    for n in range(DH // 512):
        cols = pl.ds(n * 512, 512)
        part = disc_ref[:, cols]
        total = jnp.zeros((FP, 512), f32)
        for _ in range(3):
            high = part.astype(bf16)
            total = total + mm(picked, high, NN)
            part = part - high.astype(f32)
        head_rows[:, cols] = total

    pltpu.make_async_copy(q_in.at[:, rows(g, TD)], qh.at[rows(g, TD), :], sem_q.at[0]).start()
    for i in range(16):
        for dc in (0, 1):
            if i == 0 and dc == 0:
                continue
            p = q_chip(i, 1) * 2 + (c + dc) % 2
            remote(
                q_in.at[:, rows(p, TD)], qh.at[rows(g, TD), :], sem_send.at[2], sem_q.at[i], p
            ).start()

    scale2 = math.log2(math.e) / math.sqrt(HS)
    ck = 512
    bq = 256

    def step(i_s, s_write, i_p, s_read, peak):
        if i_s is not None:
            drain(qh.at[pl.ds(0, bq), :], sem_q.at[i_s])
            rs = rows(q_chip(i_s, -1), bq)
            qb = qh[rs, :]
            top = jnp.full((bq, 128), -jnp.inf, f32)
            qwt[:, rs] = jnp.transpose(qb.astype(f32)).astype(bf16)
        if i_p is not None:
            r = rows(q_chip(i_p, -1), bq)
            l = jnp.zeros((bq, 128), f32)
        for n in range(TOK // ck):
            cols = pl.ds(n * ck, ck)
            if i_s is not None:
                sn = mm(qb, kh[cols, :], NT)
                s_write[:, cols] = sn
                for j in range(ck // 128):
                    top = jnp.maximum(top, sn[:, j * 128:(j + 1) * 128])
            if i_p is not None:
                p = jnp.exp2((s_read[:, cols] - peak) * scale2)
                for j in range(ck // 128):
                    l = l + p[:, j * 128:(j + 1) * 128]
                probs[r, cols] = p.astype(bf16)
        if i_p is not None:
            wrow[:, r] = 1.0 / jnp.sum(jnp.transpose(l), axis=0, keepdims=True)
        if i_s is not None:
            return jnp.max(top, axis=1, keepdims=True)

    drain(kh, sem_recv.at[0])
    gather_rows(v_in, vh, 1)
    peak0 = step(0, sa, None, None, None)

    @pl.loop(0, 7, init_carry=peak0)
    def fwd(i, peak):
        peak1 = step(2 * i + 1, sb, 2 * i, sa, peak)
        return step(2 * i + 2, sa, 2 * i + 1, sb, peak1)

    peak15 = step(15, sb, 14, sa, fwd)
    step(None, None, 15, sb, peak15)

    bt = 512
    inv_scale = 1.0 / math.sqrt(HS)
    mine = pl.ds(pl.multiple_of(g * HS, HS), HS)

    def pair(i):
        return rows(q_chip(2 * i, -1), bq), rows(q_chip(2 * i + 1, -1), bq)

    def load_rows(ref, i, cols=slice(None)):
        r0, r1 = pair(i)
        return jnp.concatenate([ref[r0, cols], ref[r1, cols]], axis=0)

    def load_cols(ref, i):
        r0, r1 = pair(i)
        return jnp.concatenate([ref[:, r0], ref[:, r1]], axis=1)

    def store_rows(ref, i, value):
        r0, r1 = pair(i)
        ref[r0, :] = value[:bq]
        ref[r1, :] = value[bq:]

    def row_factor(i, factor):
        return jnp.transpose(jnp.broadcast_to(load_cols(wrow, i) * factor, (HS, bt)))

    def give(src, ch, out, which):
        other = ch * 2 + (1 - c)
        same = ch * 2 + c
        remote(
            src.at[rows(other, TD), :], out.at[:, mine], sem_send.at[which], sem_recv.at[which], other
        ).start()

        @pl.when(ch != chip)
        def _():
            remote(
                src.at[rows(same, TD), :], out.at[:, mine], sem_send.at[which], sem_recv.at[which], same
            ).start()

        @pl.when(ch == chip)
        def _():
            pltpu.make_async_copy(
                src.at[rows(same, TD), :], out.at[:, mine], sem_recv.at[which]
            ).start()

    def give_pair(src, i, out, which):
        give(src, q_chip(2 * i, -1), out, which)
        give(src, q_chip(2 * i + 1, -1), out, which)

    memberl[...] = (member[...].astype(f32) * wrow[...]).astype(bf16)
    drain(vh, sem_recv.at[1])

    @pl.loop(0, TOK // (2 * bt), init_carry=jnp.zeros((FP, HS), f32))
    def pooled_sum(i, total):
        pairs = (2 * i, 2 * i + 1)
        weights = jnp.concatenate([load_rows(probs, j) for j in pairs], axis=0)
        product = mm(weights, vh[...], NN)
        for n, j in enumerate(pairs):
            o = (product[n * bt:(n + 1) * bt, :] * row_factor(j, 1.0)).astype(bf16)
            store_rows(oh, j, o)
            total = total + mm(load_cols(member, j), o, NN)

        @pl.when(i < 2)
        def _():
            for j in pairs:
                give_pair(oh, j, lat_out, 3)

        return total

    pooled = pooled_sum * inv_count
    square = jnp.sum(pooled * pooled, axis=1, keepdims=True)
    pooled_b = pooled.astype(bf16)
    for n in range(DH // 512):
        cols = pl.ds(n * 512, 512)
        rs_src[:, cols] = mm(pooled_b, w_ref[:, cols], NN).astype(bf16)
    lane_o = lax.broadcasted_iota(jnp.int32, (FP, OT), 1)

    def high_low(value):
        high = value.astype(bf16).astype(f32)
        return jnp.where(lane_o == 0, high, jnp.where(lane_o == 1, value - high, 0.0))

    rs_src[:, DH:] = high_low(square).astype(bf16)

    def owner_of(p):
        ch = p // 2
        second = jnp.where(ch % 5 == 0, 16 + ch // 5, jnp.where(ch == 4, OWN - 1, 2 * OWN))
        return jnp.where(p % 2 == 0, ch, second)

    owner = owner_of(g)

    for off in FAR:
        p = peer(off)
        o = owner_of(p)

        @pl.when(o < OWN)
        def _():
            remote(
                rs_src.at[:, rows(o, OT)], rs_recv.at[rows(g, FP), :],
                sem_send.at[4], sem_recv.at[4], p,
            ).start()

    @pl.when(owner < OWN)
    def _():
        pltpu.make_async_copy(
            rs_src.at[:, rows(owner, OT)], rs_recv.at[rows(g, FP), :], sem_recv.at[4]
        ).start()

    def frame_sums(lo, hi):
        for n in range(lo, hi):
            cols = pl.ds(n * 512, 512)
            rbuf[:, cols] = mm(memberl[...], probs[:, cols], NN).astype(bf16)

    frame_sums(0, 4)

    @pl.when(owner < OWN)
    def _():
        drain(rs_recv, sem_recv.at[4])
        total = jnp.zeros((FP, OT), f32)
        for n in range(GEN):
            total = total + rs_recv[n * FP:(n + 1) * FP, :].astype(f32)
        both = high_low(total[:, 0:1] + total[:, 1:2])
        total = jnp.where(owner == OWN - 1, both, total)
        ag_src[...] = total.astype(bf16)
        pltpu.make_async_copy(ag_src, proj.at[:, rows(owner, OT)], sem_recv.at[5]).start()
        for off in FAR:
            p = peer(off)
            remote(
                ag_src, proj.at[:, rows(owner, OT)], sem_send.at[5], sem_recv.at[5], p
            ).start()

    frame_sums(4, 8)
    drain(proj, sem_recv.at[5])

    squares = proj[:, DH:DH + 128].astype(f32)
    squares = squares[:, 0:1] + squares[:, 1:2]
    root = jnp.sqrt(squares / (GEN * HS) + EPS)
    inv_root = 1.0 / root
    score = jnp.zeros((FP, 1), f32)
    dot_sum = jnp.zeros((FP, 1), f32)
    raw = jnp.zeros((FP, HS), f32)
    for n in range(DH // 512):
        cols = pl.ds(n * 512, 512)
        hr = head_rows[:, cols]
        pre = proj[:, cols].astype(f32) * inv_root
        gate = jax.nn.sigmoid(pre)
        feature = pre * gate
        gsf[:, cols] = feature
        slope = hr * (gate + feature * (1.0 - gate))
        score = score + jnp.sum(feature * hr, axis=1, keepdims=True)
        dot_sum = dot_sum + jnp.sum(slope * pre, axis=1, keepdims=True)
        raw = raw + mm(slope.astype(bf16), w_ref[:, cols], NT)
    weight = (time_ref[0].astype(f32) + 1.0) / NSTEPS
    grad_score = -weight * jax.nn.sigmoid(-score) / FRAMES
    grad_pooled = (grad_score * inv_root) * raw
    grad_pooled = grad_pooled - (grad_score * dot_sum * inv_root * inv_root / (GEN * HS)) * pooled
    table = (TOK * (grad_pooled * inv_count)).astype(bf16)
    g_src[...] = table
    pltpu.make_async_copy(g_src, g_all.at[rows(g, FP), :], sem_recv.at[7]).start()
    for off in FAR:
        p = peer(off)
        remote(g_src, g_all.at[rows(g, FP), :], sem_send.at[7], sem_recv.at[7], p).start()

    for i in range(4, 8):
        give_pair(oh, i, lat_out, 3)
    pltpu.make_async_copy(rbuf.at[:, rows(g, TD)], r_all.at[rows(g, FP), :], sem_recv.at[6]).start()
    for off in FAR:
        p = peer(off)
        remote(
            rbuf.at[:, rows(p, TD)], r_all.at[rows(g, FP), :], sem_send.at[6], sem_recv.at[6], p
        ).start()

    first = 4
    cb = 1024
    dkt[...] = jnp.zeros_like(dkt)

    def grads_of(i):
        grad_rows = mm(load_cols(member, i), g_src[...], TN)
        delta = jnp.sum(grad_rows * load_rows(oh, i).astype(f32), axis=1, keepdims=True)
        qb = (load_cols(qwt, i).astype(f32) * (load_cols(wrow, i) * inv_scale)).astype(bf16)
        return grad_rows.astype(bf16), delta, qb

    @pl.loop(0, first)
    def _(i):
        grad_b, delta, qb = grads_of(i)
        acc = jnp.zeros((bt, HS), f32)
        for n in range(TOK // cb):
            cols = pl.ds(n * cb, cb)
            dp = mm(grad_b, vh[cols, :], NT)
            ds = (dp - delta).astype(bf16) * load_rows(probs, i, cols)
            acc = acc + mm(ds, kh[cols, :], NN)
            dkt[:, cols] += mm(qb, ds, NN)
        store_rows(qh, i, (acc * row_factor(i, inv_scale)).astype(bf16))
        give_pair(qh, i, dq_out, 9)

    def part(j, k):
        return pl.ds((2 * j + k) * HS, HS)

    def store_part(ref, j, value):
        ref[:, part(j, 0)] = value[:bq, :]
        ref[:, part(j, 1)] = value[bq:, :]

    def load_part(ref, j):
        return jnp.concatenate([ref[:, part(j, 0)], ref[:, part(j, 1)]], axis=0)

    rest = TOK // bt - first
    for j in range(rest):
        grad_b, delta, qb = grads_of(first + j)
        dob[j * bt:(j + 1) * bt, :] = grad_b
        store_part(sb, j, jnp.broadcast_to(delta, (bt, HS)))
        store_part(sa, j, jnp.zeros((bt, HS), f32))
        r0, r1 = pair(first + j)
        qwt[:, r0] = qb[:, :bq]
        qwt[:, r1] = qb[:, bq:]

    @pl.loop(0, 4)
    def _(i):
        chips = [q_chip(4 * i + m, -1) for m in range(4)]
        spans = [rows(ch, bq) for ch in chips]
        kc = jnp.concatenate([kh[r, :] for r in spans], axis=0)
        vc = jnp.concatenate([vh[r, :] for r in spans], axis=0)
        for j in range(rest):
            dp = mm(dob[j * bt:(j + 1) * bt, :], vc, NT)
            pb = jnp.concatenate([load_rows(probs, first + j, r) for r in spans], axis=1)
            ds = (dp - load_part(sb, j)[:, 0:1]).astype(bf16) * pb
            store_part(sa, j, load_part(sa, j) + mm(ds, kc, NN))
            dk = mm(load_cols(qwt, first + j), ds, NN)
            for m in range(4):
                dkt[:, spans[m]] += dk[:, m * bq:(m + 1) * bq]
        for m in range(4):
            kh[spans[m], :] = jnp.transpose(dkt[:, spans[m]]).astype(bf16)
            give(kh, chips[m], dk_out, 10)

    for j in range(rest):
        i = first + j
        store_rows(qh, i, (load_part(sa, j) * row_factor(i, inv_scale)).astype(bf16))
        give_pair(qh, i, dq_out, 9)

    for n in range(DH // 512):
        cols = pl.ds(n * 512, 512)
        value = grad_score * gsf[:, cols]
        high = value.astype(bf16)
        low = (value - high.astype(f32)).astype(bf16)
        hp_src[:, cols] = (mm(picked_t, high, NN) + mm(picked_t, low, NN)).astype(bf16)
    pltpu.make_async_copy(hp_src, hp_all.at[rows(x, 16), :], sem_recv.at[8]).start()
    for d in range(1, GRP):
        pltpu.make_async_remote_copy(
            src_ref=hp_src, dst_ref=hp_all.at[rows(x, 16), :],
            send_sem=sem_send.at[8], recv_sem=sem_recv.at[8],
            device_id={"grp": (x + d) % GRP}, device_id_type=MESH,
        ).start()

    drain(r_all, sem_recv.at[6])
    drain(g_all, sem_recv.at[7])
    for h in range(GEN):
        hr = pl.ds(h * FP, FP)
        qwt[:, h * HS:(h + 1) * HS] = mm(r_all[hr, :], g_all[hr, :], TN).astype(bf16)
    to_dv = pltpu.make_async_copy(qwt, dv_out, sem_recv.at[1])
    to_dv.start()
    drain(hp_all, sem_recv.at[8])
    total = jnp.zeros((16, DH), f32)
    for n in range(GRP):
        total = total + hp_all[n * 16:(n + 1) * 16, :].astype(f32)
    gh_out[...] = total[:NDH, :]

    to_dv.wait()
    drain(lat_out, sem_recv.at[3])
    drain(dq_out, sem_recv.at[9])
    drain(dk_out, sem_recv.at[10])
    sent = kh.at[pl.ds(0, (GEN - 1) * TD), :]
    for n in (0, 1, 2, 3, 9, 10):
        drain(sent, sem_send.at[n])

    @pl.when(owner < OWN)
    def _():
        drain(rs_src.at[:, pl.ds(0, (OWN - 1) * OT)], sem_send.at[4])
        drain(rs_recv.at[pl.ds(0, (GEN - 1) * FP), :], sem_send.at[5])

    @pl.when(owner >= OWN)
    def _():
        drain(rs_src, sem_send.at[4])

    drain(r_all.at[pl.ds(0, (GEN - 1) * FP), :], sem_send.at[6])
    drain(g_all.at[pl.ds(0, (GEN - 1) * FP), :], sem_send.at[7])
    drain(hp_all.at[pl.ds(0, (GRP - 1) * 16), :], sem_send.at[8])


def settle(*refs):
    n = 5
    ins, outs, bufs = refs[:n], refs[n:2 * n], refs[2 * n:3 * n]
    sem_in, sem_out = refs[3 * n:]
    pieces = []
    for i in range(n):
        parts = 2 if i < n - 1 else 1
        step = ins[i].shape[0] // parts
        pieces += [(i, pl.ds(j * step, step)) for j in range(parts)]
    moves = [
        (
            pltpu.make_async_copy(ins[i].at[r], bufs[i].at[r], sem_in.at[m]),
            pltpu.make_async_copy(bufs[i].at[r], outs[i].at[r], sem_out.at[m]),
        )
        for m, (i, r) in enumerate(pieces)
    ]
    for fetch, _ in moves:
        fetch.start()
    for fetch, put in moves:
        fetch.wait()
        put.start()
    for _, put in moves:
        put.wait()


def on_device(
    query_in, key_in, value_in, teacher_w, disc_heads, frame_of_token, head_of_frame, timestep
):
    vmem = pl.BlockSpec(memory_space=pltpu.VMEM)
    smem = pl.BlockSpec(memory_space=pltpu.SMEM)
    hbm = pl.BlockSpec(memory_space=pl.ANY)
    rows_shape = jax.ShapeDtypeStruct((TD, GEN * HS), bf16)
    V = pltpu.VMEM
    outs = pl.pallas_call(
        body,
        out_shape=(
            rows_shape, rows_shape, rows_shape, rows_shape,
            jax.ShapeDtypeStruct((NDH, DH), f32),
        ),
        in_specs=[hbm, hbm, hbm, vmem, vmem, vmem, smem, smem],
        out_specs=(hbm, hbm, hbm, hbm, vmem),
        scratch_shapes=[
            V((TOK, TOK), bf16),
            V((TOK, HS), bf16), V((TOK, HS), bf16), V((TOK, HS), bf16), V((TOK, HS), bf16),
            V((256, TOK), f32), V((256, TOK), f32),
            V((HS, TOK), f32), V((HS, TOK), bf16), V((1, TOK), f32),
            V((FP, TOK), bf16), V((FP, TOK), bf16), V((FP, TOK), bf16),
            V((GEN * FP, TD), bf16), V((FP, HS), bf16), V((GEN * FP, HS), bf16),
            V((FP, DH + OT), bf16), V((GEN * FP, OT), bf16), V((FP, OT), bf16),
            V((FP, DH + OT), bf16), V((FP, DH), f32), V((FP, DH), f32),
            V((16, DH), bf16), V((GRP * 16, DH), bf16),
            V((TOK // 2, HS), bf16),
            pltpu.SemaphoreType.DMA((11,)),
            pltpu.SemaphoreType.DMA((16,)),
            pltpu.SemaphoreType.DMA((11,)),
        ],
        compiler_params=pltpu.CompilerParams(
            collective_id=0, has_side_effects=True, vmem_limit_bytes=63 * 1024 * 1024
        ),
        name="clip_step",
    )(
        query_in[0], key_in[0], value_in[0], teacher_w, disc_heads,
        frame_of_token, head_of_frame, timestep,
    )
    lat, dq, dk, dv, gh = pl.pallas_call(
        settle,
        out_shape=tuple(jax.ShapeDtypeStruct(o.shape, o.dtype) for o in outs),
        in_specs=[hbm] * 5,
        out_specs=(hbm,) * 5,
        scratch_shapes=[V(o.shape, o.dtype) for o in outs] + [pltpu.SemaphoreType.DMA((9,))] * 2,
        name="settle",
    )(*outs)
    return (lat[None], dq[None], dk[None], dv[None], gh)


def solution(mesh):
    return jax.shard_map(
        on_device,
        mesh=mesh,
        in_specs=(
            P("grp", "gen", None),
            P("grp", "gen", None),
            P("grp", "gen", None),
            P("gen", None),
            P(),
            P("grp", None),
            P("grp", None),
            P("grp"),
        ),
        out_specs=(
            P("grp", "gen", None),
            P("grp", "gen", None),
            P("grp", "gen", None),
            P("grp", "gen", None),
            P(),
        ),
        check_vma=False,
    )
```
